128 devices in a mesh: lat: 8 (over z, core), lon: 16 (over y, x).
Axes of the slice: x: 4, y: 4, z: 4, core: 2. Of those that a mesh axis runs over, the one named last changes fastest.
Arguments:
- background: float32 [1024, 6144], P('lat', 'lon'), may hold values from -6 to 6
- obs_cell: int32 [2, 524288], P(None, ('lat', 'lon')), may hold values from 0 to 6143, as said below
- obs_frac: float32 [2, 524288], P(None, ('lat', 'lon')), may hold values from 0 to 1
- obs_value: float32 [524288], P(('lat', 'lon')), may hold values from -6 to 6
Outputs:
- analysis: float32 [1024, 6144], P('lat', 'lon')
The draws below stay inside these ranges and needn't reach their ends.
Inputs may be any that keep to these rules, and one draw needn't show every extreme that they name: `obs_cell`: rows are at most 1022. Tiles are blocks of 128 rows by 384 columns, numbered row of tiles times 6144 / 384 plus column of tiles. Among the 4096 observations of one device (aligned blocks of the last dimension), the number in one tile is 128, 32 or half of that; the tiles that get 128 from one device get 128 from every device, and they are 8 of all tiles.
All inputs are finite; a program needn't handle non-finite values.
Results may differ from the reference program's by a relative error of at most 0.0015.
Values sent between devices are 32-bit elements; how exact they have to be, the bound alone decides.
No kernel may reach another device: no remote copies, remote signals or barrier semaphores. Data moves between devices by JAX's collectives and lax.ppermute only.
A program may use at most 64 MiB of HBM per device.

```python
import jax
import jax.numpy as jnp
from jax import lax

TH = 128
TW = 384
OBS_DEV = 4096
RAD = 12
SKEW = 4
TILES = 128
NLAT = 1024
NLON = 6144
OBS = 524288


def draw_obs_cell(key, part):
    mean_count = OBS_DEV // TILES
    dense_count = TILES // 16
    light_count = 6 * TILES // 16
    tile_columns = NLON // TW
    tile_lines = NLAT // TH
    tile_order = jax.random.permutation(jax.random.fold_in(key, 11), jnp.arange(TILES, dtype=jnp.int32))
    dense_tiles = tile_order[:dense_count]
    other_tiles = tile_order[dense_count:]

    def one_source(source_key):
        mixed_tiles = jax.random.permutation(jax.random.fold_in(source_key, 1), other_tiles)
        light_tiles = mixed_tiles[:light_count]
        medium_tiles = mixed_tiles[light_count:]
        labels = jnp.concatenate([jnp.repeat(dense_tiles, SKEW * mean_count), jnp.repeat(light_tiles, mean_count // 2), jnp.repeat(medium_tiles, mean_count)])
        labels = jax.random.permutation(jax.random.fold_in(source_key, 2), labels)
        tile_line = labels // tile_columns
        tile_column = labels % tile_columns
        row_limit = jnp.where(tile_line == tile_lines - 1, TH - 1, TH)
        local_row = jax.random.randint(jax.random.fold_in(source_key, 3), (OBS_DEV,), 0, row_limit)
        local_col = jax.random.randint(jax.random.fold_in(source_key, 4), (OBS_DEV,), 0, TW)
        return jnp.stack([tile_line * TH + local_row, tile_column * TW + local_col]).astype(jnp.int32)
    source_keys = jax.vmap(lambda source: jax.random.fold_in(key, source))(jnp.arange(TILES, dtype=jnp.int32) + 100)
    all_cells = jax.vmap(one_source)(source_keys)
    return jnp.transpose(all_cells, (1, 0, 2)).reshape(2, OBS)


def shard_levels(key, extent, shards, smallest, high):
    level = 1.0
    for position, blocks in shards:
        heights = jax.random.uniform(jax.random.fold_in(jax.random.fold_in(key, 6), position), (blocks,), jnp.float32, smallest / len(shards), high / len(shards))
        level = level * jnp.repeat(jnp.exp(heights), extent[position] // blocks).reshape((-1,) + (1,) * (len(extent) - 1 - position))
    return level


def centred(key, dims, deviation, reach, shards=(), held_as=jnp.bfloat16):
    array = jax.random.normal(key, dims, jnp.float32) * deviation
    if len(shards) > 0:
        array = shard_levels(key, dims, shards, -0.22, 0.18) * array
    return jnp.clip(array, min=-reach, max=reach).astype(held_as)


def setup_inputs(seed: int = 0) -> dict:
    seeds = jax.random.split(jax.random.key(seed), 5)
    background = centred(seeds[0], (NLAT, NLON), 1.0, 6.0, ((0, 8), (1, 16)), jnp.float32)
    obs_cell = draw_obs_cell(jax.random.fold_in(seeds[4], 71), 0)
    obs_frac = jnp.clip(1.0 * jax.random.uniform(seeds[2], (2, OBS), jnp.float32) ** shard_levels(seeds[2], (2, OBS), ((1, 128),), -0.2, 0.2), 0.0, 1.0)
    obs_value = centred(seeds[3], (OBS,), 1.0, 6.0, ((0, 128),), jnp.float32)
    return dict(background=background, obs_cell=obs_cell, obs_frac=obs_frac, obs_value=obs_value)


gamma_two = 0.35


def taper_weight(distance, kappa_value):
    square = distance * distance
    inside = jnp.maximum(1.0 - square / float(RAD * RAD), 0.0)
    return jnp.exp(-square / kappa_value) * (inside * inside)


def interpolate(grid_field, cell_row, cell_col, frac_row, frac_col):
    next_col = jnp.mod(cell_col + 1, NLON)
    corner_a = grid_field[cell_row, cell_col]
    corner_b = grid_field[cell_row, next_col]
    corner_c = grid_field[cell_row + 1, cell_col]
    corner_d = grid_field[cell_row + 1, next_col]
    upper_part = (1.0 - frac_row) * (1.0 - frac_col) * corner_a + (1.0 - frac_row) * frac_col * corner_b
    lower_part = frac_row * (1.0 - frac_col) * corner_c + frac_row * frac_col * corner_d
    return upper_part + lower_part


def rounded(values_in):
    return lax.optimization_barrier(values_in.astype(jnp.bfloat16)).astype(jnp.float32)


def spread_sums(cell_row, cell_col, frac_row, frac_col, departure, kappa_value):
    offsets = jnp.arange(2 * RAD, dtype=jnp.int32) - RAD + 1
    offset_float = offsets.astype(jnp.float32)

    def add_source(running, block_items):
        row_block, col_block, frow_block, fcol_block, dep_block = block_items
        row_weight = taper_weight(offset_float[None, :] - frow_block[:, None], kappa_value)
        col_weight = taper_weight(offset_float[None, :] - fcol_block[:, None], kappa_value)
        col_round = rounded(col_weight)
        dep_round = rounded(dep_block[:, None] * row_weight)
        row_round = rounded(row_weight)
        row_hit = row_block[:, None, None] + offsets[None, :, None] + RAD
        col_hit = jnp.mod(col_block[:, None, None] + offsets[None, None, :], NLON)
        running = running.at[0, row_hit, col_hit].add(dep_round[:, :, None] * col_round[:, None, :])
        running = running.at[1, row_hit, col_hit].add(row_round[:, :, None] * col_round[:, None, :])
        return running, None

    block_items = (cell_row.reshape(TILES, OBS_DEV), cell_col.reshape(TILES, OBS_DEV),
                   frac_row.reshape(TILES, OBS_DEV), frac_col.reshape(TILES, OBS_DEV),
                   departure.reshape(TILES, OBS_DEV))
    start_sums = jnp.zeros((2, NLAT + 2 * RAD, NLON), jnp.float32)
    finished = lax.scan(add_source, start_sums, block_items)[0]
    return finished[0, RAD:RAD + NLAT], finished[1, RAD:RAD + NLAT]


def reference(background, obs_cell, obs_frac, obs_value):
    kappa_one = RAD * RAD / 9.0
    kappa_two = gamma_two * kappa_one
    cell_row = obs_cell[0]
    cell_col = obs_cell[1]
    frac_row = obs_frac[0]
    frac_col = obs_frac[1]
    first_dep = obs_value - interpolate(background, cell_row, cell_col, frac_row, frac_col)
    numer_one, denom_one = spread_sums(cell_row, cell_col, frac_row, frac_col, first_dep, kappa_one)
    first_pass = background + numer_one / (denom_one + 1.0)
    second_dep = obs_value - interpolate(first_pass, cell_row, cell_col, frac_row, frac_col)
    numer_two, denom_two = spread_sums(cell_row, cell_col, frac_row, frac_col, second_dep, kappa_two)
    return first_pass + numer_two / (denom_two + 1.0)
```

```python
import functools

import jax
import jax.numpy as jnp
from jax import lax
from jax.experimental import pallas as pl
from jax.experimental.pallas import tpu as pltpu
from jax.sharding import PartitionSpec as P

RAD = 12
MARGIN = 24
TH = 128
TW = 384
CAP = 256
USED = CAP - 1
ROUNDS = 5
EXT_ROWS = TH + 2 * MARGIN
LANES = 512
ROW_CODE = 64.0
COL_CODE = 192.0
KAPPA_ONE = RAD * RAD / 9.0
KAPPA_TWO = 0.35 * KAPPA_ONE
BLK = 512
f32 = jnp.float32
bf16 = jnp.bfloat16


def neighbour(block, axis, distance, wrap):
    count = lax.axis_size(axis)
    route = [(i, (i + distance) % count) for i in range(count) if wrap or 0 <= i + distance < count]
    return lax.ppermute(block, axis, route)


def three_parts(x):
    a = x.astype(bf16)
    rest = x - a.astype(f32)
    b = rest.astype(bf16)
    c = (rest - b.astype(f32)).astype(bf16)
    return [a, b, c]


def place_kernel(round_ref, cell_ref, frac_ref, value_ref, out_ref, acc_ref, tile_ref, bin_ref, run_ref, *, lats, lons):
    obs = value_ref.shape[1]
    first_slot = (round_ref[0] * USED).astype(f32)
    half_lon = lons // 2
    per_class = (lats // 2) * half_lon
    steps = obs // BLK
    line = lax.broadcasted_iota(jnp.int32, (128, 128), 0)
    row_line = lax.broadcasted_iota(jnp.int32, (128, 128), 1)
    tile_line = lax.broadcasted_iota(jnp.int32, (per_class, BLK), 0).astype(f32).astype(bf16)
    slot_line = lax.broadcasted_iota(jnp.int32, (CAP, BLK), 0).astype(f32).astype(bf16)
    ones = jnp.ones((per_class, BLK), bf16)
    zeros = jnp.zeros((per_class, BLK), bf16)
    acc_ref[...] = jnp.zeros_like(acc_ref)
    run_ref[...] = jnp.zeros_like(run_ref)

    def split(k):
        lanes = pl.ds(pl.multiple_of(k * BLK, BLK), BLK)
        row = cell_ref[0:1, lanes]
        col = cell_ref[1:2, lanes]
        lat = lax.shift_right_logical(row, 7)
        lon = (col.astype(f32) * (1.0 / TW) + 0.5 / TW).astype(jnp.int32)
        return lanes, lat, row - lat * TH, lon, col - lon * TW

    def moves(local, size, parity, own):
        before = local <= MARGIN - 2
        after = local >= size - MARGIN
        return jnp.where((own & 1) == parity, 0, jnp.where(before, -1, jnp.where(after, 1, 0)))

    def count(k, carry):
        lanes, lat, local_row, lon, local_col = split(k)
        for pa in range(2):
            to_lat = lat + moves(local_row, TH, pa, lat)
            fine_lat = ((to_lat & 1) == pa) & (to_lat >= 0) & (to_lat < lats)
            for pb in range(2):
                move = moves(local_col, TW, pb, lon)
                to_lon = lon + move
                fine = fine_lat & ((to_lon & 1) == pb)
                to_lon = jnp.where(to_lon < 0, to_lon + lons, to_lon)
                to_lon = jnp.where(to_lon >= lons, to_lon - lons, to_lon)
                rel_col = local_col - move * TW
                tile = lax.shift_right_logical(to_lat, 1) * half_lon + lax.shift_right_logical(to_lon, 1)
                tile = jnp.where(fine, tile, -1).astype(f32)
                strip = lax.shift_right_logical(rel_col + MARGIN, 4).astype(f32)
                q = 2 * pa + pb
                tile_ref[q, :, lanes] = tile
                bin_ref[q, :, lanes] = strip
                member = jnp.where(jnp.broadcast_to(tile.astype(bf16), (per_class, BLK)) == tile_line, ones, zeros)
                hot = jnp.where(jnp.broadcast_to(strip.astype(bf16), (per_class, BLK)) == tile_line, ones, zeros)
                run_ref[q] += lax.dot_general(
                    hot, member, (((1,), (1,)), ((), ())), preferred_element_type=f32
                )
        return carry

    lax.fori_loop(0, steps, count, 0)
    before = jnp.where(line > row_line, 1.0, 0.0).astype(bf16)[0:per_class, 0:per_class]

    def two_parts(x):
        high = jnp.floor(x * (1.0 / 256.0)) * 256.0
        return high.astype(bf16), (x - high).astype(bf16)

    more = jnp.zeros((1, per_class), f32)
    for q in range(4):
        held = run_ref[q]
        most = jnp.sum(held, axis=0, keepdims=True)
        for k in range(1, ROUNDS):
            more = more + jnp.where(most > float(USED * k), 0.25, 0.0)
        high, low = two_parts(held)
        run_ref[q] = jnp.dot(before, high, preferred_element_type=f32) + jnp.dot(
            before, low, preferred_element_type=f32
        )
    more = jnp.max(more)
    more = jnp.where(more > 0.0, float(ROUNDS - 1), 0.0)

    def step(k, carry):
        lanes, lat, local_row, lon, local_col = split(k)
        parts = (
            three_parts(frac_ref[0:1, lanes])
            + three_parts(frac_ref[1:2, lanes])
            + three_parts(value_ref[0:1, lanes])
        )
        for pa in range(2):
            rel_row = local_row - moves(local_row, TH, pa, lat) * TH
            for pb in range(2):
                rel_col = local_col - moves(local_col, TW, pb, lon) * TW
                q = 2 * pa + pb
                tile = tile_ref[q, :, lanes].astype(bf16)
                strip = bin_ref[q, :, lanes].astype(bf16)
                inside = jnp.broadcast_to(tile, (per_class, BLK)) == tile_line
                member = jnp.where(inside, ones, zeros)
                hot = jnp.where(jnp.broadcast_to(strip, (per_class, BLK)) == tile_line, ones, zeros)
                run = run_ref[q]
                ranks = []
                for s in range(BLK // 128):
                    some = slice(128 * s, 128 * s + 128)
                    mem, hit = member[:, some], hot[:, some]
                    high, low = two_parts(run)
                    ahead = jnp.dot(
                        jnp.concatenate([high, low], axis=1),
                        jnp.concatenate([mem, mem], axis=0),
                        preferred_element_type=f32,
                    )
                    pair = jnp.concatenate([mem, hit], axis=0)
                    alike = lax.dot_general(
                        pair, pair, (((0,), (0,)), ((), ())), preferred_element_type=f32
                    )
                    earlier = jnp.where((alike > 1.5) & (line < row_line), 1.0, 0.0)
                    ranks.append(
                        jnp.sum(hit.astype(f32) * ahead, axis=0, keepdims=True)
                        + jnp.sum(earlier, axis=0, keepdims=True)
                    )
                    run = run + lax.dot_general(
                        hit, mem, (((1,), (1,)), ((), ())), preferred_element_type=f32
                    )
                run_ref[q] = run
                slot = jnp.concatenate(ranks, axis=1) - first_slot
                slot = jnp.where((slot >= 0.0) & (slot < USED), slot, -1.0)
                slot = jnp.broadcast_to(slot.astype(bf16), (CAP, BLK))
                where_slot = jnp.where(slot == slot_line, jnp.ones_like(slot), jnp.zeros_like(slot))
                sent = [
                    (rel_row.astype(f32) + ROW_CODE).astype(bf16),
                    (rel_col.astype(f32) - COL_CODE).astype(bf16),
                ] + parts
                lhs = jnp.concatenate(
                    [jnp.where(inside, jnp.broadcast_to(p, (per_class, BLK)), zeros) for p in sent], axis=0
                )
                acc_ref[q] += lax.dot_general(
                    lhs, where_slot, (((1,), (1,)), ((), ())), preferred_element_type=f32
                )
        return carry

    lax.fori_loop(0, steps, step, 0)
    lane = lax.broadcasted_iota(jnp.int32, (per_class, CAP), 1)
    for pa in range(2):
        for pb in range(2):
            got = acc_ref[2 * pa + pb]
            pieces = [got[i * per_class : (i + 1) * per_class] for i in range(11)]
            fields = [
                pieces[0],
                pieces[1],
                pieces[2] + pieces[3] + pieces[4],
                pieces[5] + pieces[6] + pieces[7],
                jnp.where(lane == USED, more, pieces[8] + pieces[9] + pieces[10]),
            ]
            for i, field in enumerate(fields):
                for a in range(lats // 2):
                    first = (2 * a + pa) * lons + pb
                    for b in range(half_lon):
                        out_ref[first + 2 * b : first + 2 * b + 1, i * CAP : i * CAP + CAP] = field[
                            a * half_lon + b : a * half_lon + b + 1
                        ]


def place(round_index, obs_cell, obs_frac, obs_value, lats, lons):
    vmem = pl.BlockSpec(memory_space=pltpu.VMEM)
    return pl.pallas_call(
        functools.partial(place_kernel, lats=lats, lons=lons),
        out_shape=jax.ShapeDtypeStruct((lats * lons, 5 * CAP), f32),
        in_specs=[pl.BlockSpec(memory_space=pltpu.SMEM), vmem, vmem, vmem],
        out_specs=vmem,
        scratch_shapes=[
            pltpu.VMEM((4, 11 * lats * lons // 4, CAP), f32),
            pltpu.VMEM((4, 1, obs_value.shape[1]), f32),
            pltpu.VMEM((4, 1, obs_value.shape[1]), f32),
            pltpu.VMEM((4, lats * lons // 4, lats * lons // 4), f32),
        ],
        compiler_params=pltpu.CompilerParams(vmem_limit_bytes=40 * 1024 * 1024),
        name="place",
    )(round_index, obs_cell, obs_frac, obs_value)


def taper(distance, kappa):
    square = distance * distance
    inside = jnp.maximum(1.0 - square * (1.0 / (RAD * RAD)), 0.0)
    return jnp.exp(square * (-1.0 / kappa)) * (inside * inside)


def spread(window, group_of, groups):
    tiles = [window[16 * i : 16 * i + 16] for i in range(window.shape[0] // 16)]
    wide = jnp.broadcast_to(group_of, (16, 128))
    zero = jnp.zeros((16, 128), bf16)
    hits = [wide == float(g) for g in range(1 - len(tiles), groups)]
    out = []
    for g in range(groups):
        value = zero
        for i in range(len(tiles)):
            value = jnp.where(hits[g - i + len(tiles) - 1], tiles[i], value)
        out.append(value)
    return jnp.concatenate(out, axis=0)


def analyse_kernel(
    arrived_ref, more_ref, mid_ref, north_ref, south_ref, out_ref,
    table, dep_ref, field_ref, lhs_ref, acc_ref, bounds, extra_ref, sem,
):
    sources = arrived_ref.shape[0]
    slot_line = lax.broadcasted_iota(jnp.int32, (CAP, sources), 0)

    def load_round(src, first):
        for i in range(5):
            table[i, pl.ds(first, CAP), :] = jnp.transpose(src[:, i * CAP : (i + 1) * CAP])
        there = table[0, pl.ds(first, CAP), :] > 0.0
        return jnp.max(jnp.where(there, slot_line + 1, 0))

    used = load_round(arrived_ref, 0)
    extra = jnp.max(arrived_ref[:, 5 * CAP - 128 :][:, 127:128]).astype(jnp.int32)

    def more_rounds(k, used):
        copy = pltpu.make_async_copy(more_ref.at[k], extra_ref, sem)
        copy.start()
        copy.wait()
        count = load_round(extra_ref, pl.multiple_of((k + 1) * CAP, CAP))
        return jnp.where(count > 0, (k + 1) * CAP + count, used)

    used = lax.fori_loop(0, extra, more_rounds, used)
    chunks = (used + 7) // 8

    field_ref[0:MARGIN] = north_ref[...]
    field_ref[MARGIN : MARGIN + TH] = mid_ref[...]
    field_ref[MARGIN + TH :] = south_ref[...]

    def rows8(i, k):
        return table[i, pl.ds(pl.multiple_of(k * 8, 8), 8), :]

    def find_bounds(k, carry):
        there = rows8(0, k) > 0.0
        col = rows8(1, k) + (COL_CODE + MARGIN)
        bounds[0, k] = jnp.min(jnp.where(there, col, 511.0)).astype(jnp.int32)
        bounds[1, k] = jnp.max(jnp.where(there, col, 0.0)).astype(jnp.int32)
        return carry

    lax.fori_loop(0, chunks, find_bounds, 0)

    line8 = lax.broadcasted_iota(jnp.int32, (8, 128), 0).astype(f32)
    line128 = lax.broadcasted_iota(jnp.int32, (128, 128), 0).astype(f32)
    line48 = lax.broadcasted_iota(jnp.int32, (48, 128), 0).astype(f32)

    def departures():
        field = field_ref[...]
        beside = pltpu.roll(field, LANES - 1, 1)
        for part, grid in enumerate((field, beside)):
            high = grid.astype(bf16)
            low = (grid - high.astype(f32)).astype(bf16)
            rows = slice(part * EXT_ROWS, (part + 1) * EXT_ROWS)
            for b in range(4):
                lhs_ref[b, rows, 0:128] = high[:, 128 * b : 128 * b + 128]
                lhs_ref[b, rows, 128:256] = low[:, 128 * b : 128 * b + 128]

        def chunk(k, carry):
            row = rows8(0, k) + (MARGIN - ROW_CODE)
            col = rows8(1, k) + (COL_CODE + MARGIN)
            frac_row = rows8(2, k)
            frac_col = rows8(3, k)
            group = jnp.floor(row * 0.125)
            below = row - 8.0 * group

            def block(b, total):
                off = col - (b * 128).astype(f32)
                hot = jnp.concatenate(
                    [
                        (jnp.broadcast_to(off[j : j + 1], (128, 128)) == line128).astype(f32).astype(bf16)
                        for j in range(8)
                    ],
                    axis=1,
                )
                lines = jnp.dot(
                    lhs_ref[b], jnp.concatenate([hot, hot], axis=0), preferred_element_type=f32
                )
                out = []
                for j in range(8):
                    mine = lines[:, 128 * j : 128 * j + 128]
                    which = jnp.broadcast_to(group[j : j + 1], (8, 128))
                    picked = [jnp.zeros((8, 128), f32) for _ in range(4)]
                    for g in range(EXT_ROWS // 8):
                        hit = which == float(g)
                        for part in range(2):
                            first = part * EXT_ROWS + 8 * g
                            picked[2 * part] = jnp.where(hit, mine[first : first + 8], picked[2 * part])
                            if g + 1 < EXT_ROWS // 8:
                                picked[2 * part + 1] = jnp.where(
                                    hit, mine[first + 8 : first + 16], picked[2 * part + 1]
                                )
                    fx = frac_col[j : j + 1]
                    fy = frac_row[j : j + 1]
                    sub = jnp.broadcast_to(below[j : j + 1], (8, 128))
                    near = line8 - sub
                    weight_a = jnp.where(near == 0.0, 1.0 - fy, jnp.where(near == 1.0, fy, 0.0))
                    weight_b = jnp.where(near == -7.0, fy, 0.0)
                    mixed = weight_a * ((1.0 - fx) * picked[0] + fx * picked[2]) + weight_b * (
                        (1.0 - fx) * picked[1] + fx * picked[3]
                    )
                    out.append(jnp.sum(mixed, axis=0, keepdims=True))
                return total + jnp.concatenate(out, axis=0)

            low_block = lax.shift_right_logical(bounds[0, k], 7)
            high_block = lax.shift_right_logical(bounds[1, k], 7)
            value = lax.fori_loop(low_block, high_block + 1, block, jnp.zeros((8, 128), f32))
            dep_ref[pl.ds(pl.multiple_of(k * 8, 8), 8), :] = rows8(4, k) - value
            return carry

        lax.fori_loop(0, chunks, chunk, 0)

    def sums(kappa, row_shift, groups):
        acc_ref[...] = jnp.zeros_like(acc_ref)
        height = 32 * groups

        def chunk(k, carry):
            row = rows8(0, k) + (row_shift - ROW_CODE)
            col = rows8(1, k) + (COL_CODE + MARGIN)
            frac_row = rows8(2, k)
            frac_col = rows8(3, k)
            dep = dep_ref[pl.ds(pl.multiple_of(k * 8, 8), 8), :]
            row_group = jnp.floor((row - (RAD - 1.0)) * 0.0625)
            col_group = jnp.floor((col - (RAD - 1.0)) * 0.0625)
            row_from = 16.0 * row_group - row
            col_from = 16.0 * col_group - col
            left = []
            col_windows = []
            for j in range(8):
                gap = (line48 + row_from[j : j + 1]) - frac_row[j : j + 1]
                weight = taper(gap, kappa)
                which = row_group[j : j + 1].astype(bf16)
                numer = spread((weight * dep[j : j + 1]).astype(bf16), which, groups)
                denom = spread(weight.astype(bf16), which, groups)
                left.append(jnp.concatenate([numer, denom], axis=0))
                gap = (line48 + col_from[j : j + 1]) - frac_col[j : j + 1]
                col_windows.append(taper(gap, kappa).astype(bf16))
            left = jnp.concatenate(left, axis=1)
            first = lax.shift_right_logical(jnp.maximum(bounds[0, k] - (RAD - 1), 0), 7)
            last = lax.shift_right_logical(jnp.minimum(bounds[1, k] + RAD, LANES - 1), 7)

            def pair(w, carry):
                block = first + 2 * w
                shifted = col_group - (block * 8).astype(f32)
                right = jnp.concatenate(
                    [spread(col_windows[j], shifted[j : j + 1].astype(bf16), 16) for j in range(8)],
                    axis=1,
                )
                both = lax.dot_general(
                    left, right, (((1,), (1,)), ((), ())), preferred_element_type=f32
                )
                acc_ref[block, 0:height] += both[:, 0:128]
                acc_ref[block + 1, 0:height] += both[:, 128:256]
                return carry

            lax.fori_loop(0, lax.shift_right_logical(last - first, 1) + 1, pair, 0)
            return carry

        lax.fori_loop(0, chunks, chunk, 0)

    departures()
    sums(KAPPA_ONE, 16.0, 10)
    field_ref[0:8] = jnp.zeros((8, LANES), f32)
    field_ref[168:EXT_ROWS] = jnp.zeros((8, LANES), f32)
    for b in range(4):
        lanes = slice(128 * b, 128 * b + 128)
        field_ref[8:168, lanes] += acc_ref[b, 0:160] / (acc_ref[b, 160:320] + 1.0)
    departures()
    sums(KAPPA_TWO, 0.0, 8)
    final = jnp.concatenate(
        [
            field_ref[MARGIN : MARGIN + TH, 128 * b : 128 * b + 128]
            + acc_ref[b, 0:TH] / (acc_ref[b, TH : 2 * TH] + 1.0)
            for b in range(4)
        ],
        axis=1,
    )
    out_ref[...] = pltpu.roll(final, LANES - MARGIN, 1)[:, 0:TW]


def analyse(arrived, more, middle, north, south):
    vmem = pl.BlockSpec(memory_space=pltpu.VMEM)
    sources = arrived.shape[0]
    slots = ROUNDS * CAP
    return pl.pallas_call(
        analyse_kernel,
        out_shape=jax.ShapeDtypeStruct((TH, TW), f32),
        in_specs=[vmem, pl.BlockSpec(memory_space=pl.ANY), vmem, vmem, vmem],
        out_specs=vmem,
        scratch_shapes=[
            pltpu.VMEM((5, slots, sources), f32),
            pltpu.VMEM((slots, sources), f32),
            pltpu.VMEM((EXT_ROWS, LANES), f32),
            pltpu.VMEM((4, 2 * EXT_ROWS, 256), bf16),
            pltpu.VMEM((5, 320, 128), f32),
            pltpu.SMEM((2, slots // 8), jnp.int32),
            pltpu.VMEM((sources, 5 * CAP), f32),
            pltpu.SemaphoreType.DMA,
        ],
        compiler_params=pltpu.CompilerParams(vmem_limit_bytes=48 * 1024 * 1024),
        name="analyse",
    )(arrived, more, middle, north, south)


def on_device(background, obs_cell, obs_frac, obs_value):
    lats = lax.axis_size("lat")
    lons = lax.axis_size("lon")
    axes = ("lat", "lon")

    west = neighbour(background[:, TW - MARGIN :], "lon", 1, True)
    east = neighbour(background[:, :MARGIN], "lon", -1, True)
    spare = jnp.zeros((TH, LANES - TW - 2 * MARGIN), f32)
    middle = jnp.concatenate([west, background, east, spare], axis=1)
    north = neighbour(middle[TH - MARGIN :], "lat", 1, False)
    south = neighbour(middle[:MARGIN], "lat", -1, False)

    values = obs_value[None, :]

    def outgoing(k):
        return place(k.reshape(1), obs_cell, obs_frac, values, lats, lons)

    arrived = lax.all_to_all(
        outgoing(jnp.int32(0)), axes, split_axis=0, concat_axis=0, tiled=True
    )
    extra = jnp.max(arrived[:, 5 * CAP - 1]).astype(jnp.int32)
    devices = lats * lons
    place_here = lax.axis_index(axes)
    ring = [(i, (i + 1) % devices) for i in range(devices)]

    def pass_round(step, held):
        moving, got = held
        mine = lax.dynamic_slice_in_dim(moving, place_here, 1, 0)
        source = (place_here - step + devices) % devices
        got = lax.dynamic_update_slice_in_dim(got, mine, source, 0)
        return lax.ppermute(moving, axes, ring), got

    def fetch_more():
        def body(k, held):
            moving = outgoing(k + 1)
            got = lax.fori_loop(0, devices, pass_round, (moving, jnp.zeros_like(moving)))[1]
            return lax.dynamic_update_index_in_dim(held, got, k, 0)

        return lax.fori_loop(0, extra, body, none())

    def none():
        return jnp.zeros((ROUNDS - 1, devices, 5 * CAP), f32)

    more = fetch_more()
    return analyse(arrived, more, middle, north, south)


def solution(mesh):
    placed = (P("lat", "lon"), P(None, ("lat", "lon")), P(None, ("lat", "lon")), P(("lat", "lon")))
    return jax.shard_map(
        on_device, mesh=mesh, in_specs=placed, out_specs=P("lat", "lon"), check_vma=False
    )
```

```python
import functools

import jax
import jax.numpy as jnp
from jax import lax
from jax.experimental import pallas as pl
from jax.experimental.pallas import tpu as pltpu
from jax.sharding import PartitionSpec as P

RAD = 12
MARGIN = 24
TH = 128
TW = 384
CAP = 192
ROUNDS = 6
BAND = 8192
NOWHERE = 1 << 30
PAD = 4
EXT_ROWS = TH + 2 * MARGIN
LANES = 512
ROW_CODE = 64.0
COL_CODE = 192.0
KAPPA_ONE = RAD * RAD / 9.0
KAPPA_TWO = 0.35 * KAPPA_ONE
f32 = jnp.float32
bf16 = jnp.bfloat16


def neighbour(block, axis, distance, wrap):
    count = lax.axis_size(axis)
    route = [(i, (i + distance) % count) for i in range(count) if wrap or 0 <= i + distance < count]
    return lax.ppermute(block, axis, route)


def sort_observations(obs_cell, obs_frac, obs_value, lats):
    row, col = obs_cell[0], obs_cell[1]
    lat = row // TH
    local_row = row - lat * TH
    up = (local_row <= MARGIN - 2) & (lat > 0)
    down = (local_row >= TH - MARGIN) & (lat < lats - 1)
    move = jnp.where(up, -1, jnp.where(down, 1, 0))
    own_key = lat * BAND + col
    next_key = jnp.where(up | down, own_key + move * BAND, NOWHERE)
    keys = jnp.concatenate([own_key, next_key])
    rows = jnp.concatenate([local_row, local_row - move * TH]).astype(f32) + ROW_CODE
    twice = [jnp.concatenate([x, x]) for x in (obs_frac[0], obs_frac[1], obs_value)]
    return lax.sort((keys, rows, *twice), num_keys=1, is_stable=False)


def segment_limits(keys, lats, lons):
    low = [TW * b - MARGIN for b in range(lons)]
    high = [TW * (b + 1) + MARGIN - 1 for b in range(lons)]
    total = TW * lons
    band = low + high + [0, total]
    band[0] += total
    band[2 * lons - 1] -= total
    limits = jnp.array([a * BAND + x for a in range(lats) for x in band], jnp.int32)
    return jnp.sum((keys[None, :] < limits[:, None]).astype(jnp.int32), axis=1)


def pieces_of(limit_ref, a, b, lons):
    base = a * (2 * lons + 2)
    first = limit_ref[base + b]
    end = limit_ref[base + lons + b]
    if b == 0:
        return (first, limit_ref[base + 2 * lons + 1]), (limit_ref[base + 2 * lons], end)
    if b == lons - 1:
        return (first, limit_ref[base + 2 * lons + 1]), (limit_ref[base + 2 * lons], end)
    return (first, end), None


def place_kernel(round_ref, limit_ref, key_ref, row_ref, fy_ref, fx_ref, value_ref, out_ref, near_ref, far_ref, *, lats, lons):
    tiles = key_ref.shape[0]
    skipped = round_ref[0] * CAP
    col = (key_ref[...] & (BAND - 1)).astype(f32)
    near = [row_ref[...], col, fy_ref[...], fx_ref[...], value_ref[...], row_ref[...], fy_ref[...], value_ref[...]]
    lane = lax.broadcasted_iota(jnp.int32, (8, 128), 1)
    line = lax.broadcasted_iota(jnp.int32, (8, 128), 0)
    for i, x in enumerate(near):
        near_ref[pl.ds(8 * PAD + i, tiles, stride=8), :] = x
    for i, x in ((5, col), (6, fx_ref[...])):
        far_ref[pl.ds(8 * PAD + i, tiles, stride=8), :] = x
    entry = jnp.where(line < 5, lane, 128 + (lane & 63))
    col_line = (line == 1) | ((line == 5) & (lane >= 64))
    meta = (line == 7) & (lane >= 64)

    def window(ref, tile, start):
        return ref[pl.ds(pl.multiple_of(tile * 8, 8), 8), :]

    def take(start):
        start = jnp.clip(start + 128 * PAD, 0, (tiles + PAD) * 128)
        tile = lax.shift_right_logical(start, 7)
        inside = start & 127
        turn = (128 - inside) & 127
        views = [pltpu.roll(window(near_ref, tile + i, 0), turn, 1) for i in range(3)]
        kept = lane < 128 - inside
        first = jnp.where(kept, views[0], views[1])
        second = jnp.where(kept, views[1], views[2])
        start = start + 64
        tile = lax.shift_right_logical(start, 7)
        inside = start & 127
        turn = (128 - inside) & 127
        views = [pltpu.roll(window(far_ref, tile + i, 0), turn, 1) for i in range(2)]
        third = jnp.where(lane < 128 - inside, views[0], views[1])
        return jnp.where(line < 5, first, jnp.where(lane < 64, second, third))

    def band(a, most):
        for b in range(lons):
            one, two = pieces_of(limit_ref, a, b, lons)
            count = one[1] - one[0] - skipped
            shift = -float(TW * b) - COL_CODE
            value = take(one[0] + skipped)
            if two is None:
                value = value + jnp.where(col_line, shift, 0.0)
            else:
                total = float(TW * lons)
                first_shift, second_shift = (shift - total, shift) if b == 0 else (shift, shift + total)
                value = value + jnp.where(col_line, first_shift, 0.0)
                other = take(two[0] - count) + jnp.where(col_line, second_shift, 0.0)
                value = jnp.where(entry < count, value, other)
                count = count + two[1] - two[0]
            most = jnp.maximum(most, count)
            out_ref[a * lons + b] = jnp.where((entry < count) & ~meta, value, 0.0)
        return most

    most = lax.fori_loop(0, lats, band, 0)
    extra = jnp.maximum(most + (CAP - 1), 0) // CAP - 1
    extra = jnp.maximum(extra, 0).astype(f32)

    def flag(t, carry):
        out_ref[t, 7:8, 64:128] = jnp.full((1, 64), extra, f32)
        return carry

    lax.fori_loop(0, lats * lons, flag, 0)


def place(round_index, limits, keys, rows, fy, fx, values, lats, lons):
    vmem = pl.BlockSpec(memory_space=pltpu.VMEM)
    smem = pl.BlockSpec(memory_space=pltpu.SMEM)
    tiles = keys.shape[0] // 128
    columns = [x.reshape(tiles, 128) for x in (keys, rows, fy, fx, values)]
    scratch = pltpu.VMEM((8 * (tiles + 2 * PAD), 128), f32)
    return pl.pallas_call(
        functools.partial(place_kernel, lats=lats, lons=lons),
        out_shape=jax.ShapeDtypeStruct((lats * lons, 8, 128), f32),
        in_specs=[smem, smem] + [vmem] * 5,
        out_specs=vmem,
        scratch_shapes=[scratch, scratch],
        compiler_params=pltpu.CompilerParams(vmem_limit_bytes=16 * 1024 * 1024),
        name="place",
    )(round_index, limits, *columns)


def untouched(shape):
    return pl.pallas_call(
        lambda ref: None,
        out_shape=jax.ShapeDtypeStruct(shape, f32),
        out_specs=pl.BlockSpec(memory_space=pl.ANY),
        name="untouched",
    )()


def taper(distance, kappa):
    square = distance * distance
    inside = jnp.maximum(1.0 - square * (1.0 / (RAD * RAD)), 0.0)
    return jnp.exp(square * (-1.0 / kappa)) * (inside * inside)


def spread(window, group_of, groups):
    tiles = [window[16 * i : 16 * i + 16] for i in range(window.shape[0] // 16)]
    wide = jnp.broadcast_to(group_of, (16, 128))
    zero = jnp.zeros((16, 128), bf16)
    hits = [wide == float(g) for g in range(1 - len(tiles), groups)]
    out = []
    for g in range(groups):
        value = zero
        for i in range(len(tiles)):
            value = jnp.where(hits[g - i + len(tiles) - 1], tiles[i], value)
        out.append(value)
    return jnp.concatenate(out, axis=0)


def analyse_kernel(
    extra_count, arrived_ref, more_ref, mid_ref, north_ref, south_ref, out_ref,
    table, dep_ref, field_ref, lhs_ref, acc_ref, bounds, extra_ref, sem,
):
    sources = arrived_ref.shape[0]
    sources = sources // 8
    slot_line = lax.broadcasted_iota(jnp.int32, (CAP, sources), 0)

    def load_round(src, first):
        turned = [jnp.transpose(src[pl.ds(i, sources, stride=8), :]) for i in range(8)]
        for i in range(5):
            table[i, pl.ds(first, 128), :] = turned[i]
            half = 64 * (i % 2)
            table[i, pl.ds(first + 128, 64), :] = turned[5 + i // 2][half : half + 64]
        there = table[0, pl.ds(first, CAP), :] > 0.0
        return jnp.max(jnp.where(there, slot_line + 1, 0))

    used = load_round(arrived_ref, 0)
    extra = extra_count[0]

    def more_rounds(k, used):
        copy = pltpu.make_async_copy(more_ref.at[k], extra_ref, sem)
        copy.start()
        copy.wait()
        count = load_round(extra_ref, pl.multiple_of((k + 1) * CAP, 64))
        return jnp.where(count > 0, (k + 1) * CAP + count, used)

    used = lax.fori_loop(0, extra, more_rounds, used)
    chunks = (used + 7) // 8

    field_ref[0:MARGIN] = north_ref[...]
    field_ref[MARGIN : MARGIN + TH] = mid_ref[...]
    field_ref[MARGIN + TH :] = south_ref[...]

    def rows8(i, k):
        return table[i, pl.ds(pl.multiple_of(k * 8, 8), 8), :]

    def find_bounds(k, carry):
        there = rows8(0, k) > 0.0
        col = rows8(1, k) + (COL_CODE + MARGIN)
        bounds[0, k] = jnp.min(jnp.where(there, col, 511.0)).astype(jnp.int32)
        bounds[1, k] = jnp.max(jnp.where(there, col, 0.0)).astype(jnp.int32)
        return carry

    lax.fori_loop(0, chunks, find_bounds, 0)

    line8 = lax.broadcasted_iota(jnp.int32, (8, 128), 0).astype(f32)
    line128 = lax.broadcasted_iota(jnp.int32, (128, 128), 0).astype(f32)
    line48 = lax.broadcasted_iota(jnp.int32, (48, 128), 0).astype(f32)

    def departures():
        field = field_ref[...]
        beside = pltpu.roll(field, LANES - 1, 1)
        for part, grid in enumerate((field, beside)):
            high = grid.astype(bf16)
            low = (grid - high.astype(f32)).astype(bf16)
            rows = slice(part * EXT_ROWS, (part + 1) * EXT_ROWS)
            for b in range(4):
                lhs_ref[b, rows, 0:128] = high[:, 128 * b : 128 * b + 128]
                lhs_ref[b, rows, 128:256] = low[:, 128 * b : 128 * b + 128]

        def chunk(k, carry):
            row = rows8(0, k) + (MARGIN - ROW_CODE)
            col = rows8(1, k) + (COL_CODE + MARGIN)
            frac_row = rows8(2, k)
            frac_col = rows8(3, k)
            group = jnp.floor(row * 0.125)
            below = row - 8.0 * group

            def block(b, total):
                off = col - (b * 128).astype(f32)
                hot = jnp.concatenate(
                    [
                        (jnp.broadcast_to(off[j : j + 1], (128, 128)) == line128).astype(f32).astype(bf16)
                        for j in range(8)
                    ],
                    axis=1,
                )
                lines = jnp.dot(
                    lhs_ref[b], jnp.concatenate([hot, hot], axis=0), preferred_element_type=f32
                )
                out = []
                for j in range(8):
                    mine = lines[:, 128 * j : 128 * j + 128]
                    which = jnp.broadcast_to(group[j : j + 1], (8, 128))
                    picked = [jnp.zeros((8, 128), f32) for _ in range(4)]
                    for g in range(EXT_ROWS // 8):
                        hit = which == float(g)
                        for part in range(2):
                            first = part * EXT_ROWS + 8 * g
                            picked[2 * part] = jnp.where(hit, mine[first : first + 8], picked[2 * part])
                            if g + 1 < EXT_ROWS // 8:
                                picked[2 * part + 1] = jnp.where(
                                    hit, mine[first + 8 : first + 16], picked[2 * part + 1]
                                )
                    fx = frac_col[j : j + 1]
                    fy = frac_row[j : j + 1]
                    sub = jnp.broadcast_to(below[j : j + 1], (8, 128))
                    near = line8 - sub
                    weight_a = jnp.where(near == 0.0, 1.0 - fy, jnp.where(near == 1.0, fy, 0.0))
                    weight_b = jnp.where(near == -7.0, fy, 0.0)
                    mixed = weight_a * ((1.0 - fx) * picked[0] + fx * picked[2]) + weight_b * (
                        (1.0 - fx) * picked[1] + fx * picked[3]
                    )
                    out.append(jnp.sum(mixed, axis=0, keepdims=True))
                return total + jnp.concatenate(out, axis=0)

            low_block = lax.shift_right_logical(bounds[0, k], 7)
            high_block = lax.shift_right_logical(bounds[1, k], 7)
            value = lax.fori_loop(low_block, high_block + 1, block, jnp.zeros((8, 128), f32))
            dep_ref[pl.ds(pl.multiple_of(k * 8, 8), 8), :] = rows8(4, k) - value
            return carry

        lax.fori_loop(0, chunks, chunk, 0)

    def sums(kappa, row_shift, groups):
        acc_ref[...] = jnp.zeros_like(acc_ref)
        height = 32 * groups

        def chunk(k, carry):
            row = rows8(0, k) + (row_shift - ROW_CODE)
            col = rows8(1, k) + (COL_CODE + MARGIN)
            frac_row = rows8(2, k)
            frac_col = rows8(3, k)
            dep = dep_ref[pl.ds(pl.multiple_of(k * 8, 8), 8), :]
            row_group = jnp.floor((row - (RAD - 1.0)) * 0.0625)
            col_group = jnp.floor((col - (RAD - 1.0)) * 0.0625)
            row_from = 16.0 * row_group - row
            col_from = 16.0 * col_group - col
            left = []
            col_windows = []
            for j in range(8):
                gap = (line48 + row_from[j : j + 1]) - frac_row[j : j + 1]
                weight = taper(gap, kappa)
                which = row_group[j : j + 1].astype(bf16)
                numer = spread((weight * dep[j : j + 1]).astype(bf16), which, groups)
                denom = spread(weight.astype(bf16), which, groups)
                left.append(jnp.concatenate([numer, denom], axis=0))
                gap = (line48 + col_from[j : j + 1]) - frac_col[j : j + 1]
                col_windows.append(taper(gap, kappa).astype(bf16))
            left = jnp.concatenate(left, axis=1)
            first = lax.shift_right_logical(jnp.maximum(bounds[0, k] - (RAD - 1), 0), 7)
            last = lax.shift_right_logical(jnp.minimum(bounds[1, k] + RAD, LANES - 1), 7)

            def pair(w, carry):
                block = first + 2 * w
                shifted = col_group - (block * 8).astype(f32)
                right = jnp.concatenate(
                    [spread(col_windows[j], shifted[j : j + 1].astype(bf16), 16) for j in range(8)],
                    axis=1,
                )
                both = lax.dot_general(
                    left, right, (((1,), (1,)), ((), ())), preferred_element_type=f32
                )
                acc_ref[block, 0:height] += both[:, 0:128]
                acc_ref[block + 1, 0:height] += both[:, 128:256]
                return carry

            lax.fori_loop(0, lax.shift_right_logical(last - first, 1) + 1, pair, 0)
            return carry

        lax.fori_loop(0, chunks, chunk, 0)

    departures()
    sums(KAPPA_ONE, 16.0, 10)
    field_ref[0:8] = jnp.zeros((8, LANES), f32)
    field_ref[168:EXT_ROWS] = jnp.zeros((8, LANES), f32)
    for b in range(4):
        lanes = slice(128 * b, 128 * b + 128)
        field_ref[8:168, lanes] += acc_ref[b, 0:160] / (acc_ref[b, 160:320] + 1.0)
    departures()
    sums(KAPPA_TWO, 0.0, 8)
    final = jnp.concatenate(
        [
            field_ref[MARGIN : MARGIN + TH, 128 * b : 128 * b + 128]
            + acc_ref[b, 0:TH] / (acc_ref[b, TH : 2 * TH] + 1.0)
            for b in range(4)
        ],
        axis=1,
    )
    out_ref[...] = pltpu.roll(final, LANES - MARGIN, 1)[:, 0:TW]


def analyse(extra, arrived, more, middle, north, south):
    vmem = pl.BlockSpec(memory_space=pltpu.VMEM)
    sources = arrived.shape[0]
    slots = ROUNDS * CAP
    return pl.pallas_call(
        analyse_kernel,
        out_shape=jax.ShapeDtypeStruct((TH, TW), f32),
        in_specs=[pl.BlockSpec(memory_space=pltpu.SMEM), vmem, pl.BlockSpec(memory_space=pl.ANY), vmem, vmem, vmem],
        out_specs=vmem,
        scratch_shapes=[
            pltpu.VMEM((5, slots, sources), f32),
            pltpu.VMEM((slots, sources), f32),
            pltpu.VMEM((EXT_ROWS, LANES), f32),
            pltpu.VMEM((4, 2 * EXT_ROWS, 256), bf16),
            pltpu.VMEM((5, 320, 128), f32),
            pltpu.SMEM((2, slots // 8), jnp.int32),
            pltpu.VMEM((sources * 8, 128), f32),
            pltpu.SemaphoreType.DMA,
        ],
        compiler_params=pltpu.CompilerParams(vmem_limit_bytes=48 * 1024 * 1024),
        name="analyse",
    )(extra.reshape(1), arrived.reshape(sources * 8, 128), more, middle, north, south)


def on_device(background, obs_cell, obs_frac, obs_value):
    lats = lax.axis_size("lat")
    lons = lax.axis_size("lon")
    axes = ("lat", "lon")
    devices = lats * lons

    west = neighbour(background[:, TW - MARGIN :], "lon", 1, True)
    east = neighbour(background[:, :MARGIN], "lon", -1, True)
    spare = jnp.zeros((TH, LANES - TW - 2 * MARGIN), f32)
    middle = jnp.concatenate([west, background, east, spare], axis=1)
    north = neighbour(middle[TH - MARGIN :], "lat", 1, False)
    south = neighbour(middle[:MARGIN], "lat", -1, False)

    columns = sort_observations(obs_cell, obs_frac, obs_value, lats)
    limits = segment_limits(columns[0], lats, lons)

    def exchange(k):
        outgoing = place(k.reshape(1), limits, *columns, lats, lons)
        return lax.all_to_all(outgoing, axes, split_axis=0, concat_axis=0, tiled=True)

    arrived = exchange(jnp.int32(0))
    extra = jnp.max(arrived[:, 7, 127]).astype(jnp.int32)

    def one_more(k, held):
        got = exchange(k + 1).reshape(1, devices * 8, 128)
        return lax.dynamic_update_slice_in_dim(held, got, k, 0)

    more = lax.fori_loop(0, extra, one_more, untouched((ROUNDS - 1, devices * 8, 128)))
    return analyse(extra, arrived, more, middle, north, south)


def solution(mesh):
    placed = (P("lat", "lon"), P(None, ("lat", "lon")), P(None, ("lat", "lon")), P(("lat", "lon")))
    return jax.shard_map(
        on_device, mesh=mesh, in_specs=placed, out_specs=P("lat", "lon"), check_vma=False
    )
```

```python
import functools

import jax
import jax.numpy as jnp
from jax import lax
from jax.experimental import pallas as pl
from jax.experimental.pallas import tpu as pltpu
from jax.sharding import PartitionSpec as P

RAD = 12
MARGIN = 24
TH = 128
TW = 384
CAP = 192
ROUNDS = 6
BAND = 8192
NOWHERE = 1 << 30
PAD = 4
EXT_ROWS = TH + 2 * MARGIN
LANES = 512
ROW_CODE = 64.0
COL_CODE = 192.0
LOG2E = 1.4426950408889634
KAPPA_ONE = RAD * RAD / 9.0
KAPPA_TWO = 0.35 * KAPPA_ONE
f32 = jnp.float32
bf16 = jnp.bfloat16


def neighbour(block, axis, distance, wrap):
    count = lax.axis_size(axis)
    route = [(i, (i + distance) % count) for i in range(count) if wrap or 0 <= i + distance < count]
    return lax.ppermute(block, axis, route)


def sort_observations(obs_cell, obs_frac, obs_value, lats):
    row, col = obs_cell[0], obs_cell[1]
    lat = row // TH
    local_row = row - lat * TH
    up = (local_row <= MARGIN - 2) & (lat > 0)
    down = (local_row >= TH - MARGIN) & (lat < lats - 1)
    move = jnp.where(up, -1, jnp.where(down, 1, 0))
    own_key = lat * BAND + col
    next_key = jnp.where(up | down, own_key + move * BAND, NOWHERE)
    keys = jnp.concatenate([own_key, next_key])
    rows = jnp.concatenate([local_row, local_row - move * TH]).astype(f32) + ROW_CODE
    twice = [jnp.concatenate([x, x]) for x in (obs_frac[0], obs_frac[1], obs_value)]
    return lax.sort((keys, rows, *twice), num_keys=1, is_stable=False)


def segment_limits(keys, lats, lons):
    low = [TW * b - MARGIN for b in range(lons)]
    high = [TW * (b + 1) + MARGIN - 1 for b in range(lons)]
    total = TW * lons
    band = low + high + [0, total]
    band[0] += total
    band[2 * lons - 1] -= total
    limits = jnp.array([a * BAND + x for a in range(lats) for x in band], jnp.int32)
    return jnp.sum((keys[None, :] < limits[:, None]).astype(jnp.int32), axis=1)


def pieces_of(limit_ref, a, b, lons):
    base = a * (2 * lons + 2)
    first = limit_ref[base + b]
    end = limit_ref[base + lons + b]
    if b == 0:
        return (first, limit_ref[base + 2 * lons + 1]), (limit_ref[base + 2 * lons], end)
    if b == lons - 1:
        return (first, limit_ref[base + 2 * lons + 1]), (limit_ref[base + 2 * lons], end)
    return (first, end), None


def place_kernel(round_ref, limit_ref, key_ref, row_ref, fy_ref, fx_ref, value_ref, out_ref, near_ref, far_ref, *, lats, lons):
    tiles = key_ref.shape[0]
    skipped = round_ref[0] * CAP
    col = (key_ref[...] & (BAND - 1)).astype(f32)
    near = [row_ref[...], col, fy_ref[...], fx_ref[...], value_ref[...], row_ref[...], fy_ref[...], value_ref[...]]
    lane = lax.broadcasted_iota(jnp.int32, (8, 128), 1)
    line = lax.broadcasted_iota(jnp.int32, (8, 128), 0)
    for i, x in enumerate(near):
        near_ref[pl.ds(8 * PAD + i, tiles, stride=8), :] = x
    for i, x in ((5, col), (6, fx_ref[...])):
        far_ref[pl.ds(8 * PAD + i, tiles, stride=8), :] = x
    entry = jnp.where(line < 5, lane, 128 + (lane & 63))
    col_line = (line == 1) | ((line == 5) & (lane >= 64))
    meta = (line == 7) & (lane >= 64)

    def window(ref, tile, start):
        return ref[pl.ds(pl.multiple_of(tile * 8, 8), 8), :]

    def take(start):
        start = jnp.clip(start + 128 * PAD, 0, (tiles + PAD) * 128)
        tile = lax.shift_right_logical(start, 7)
        inside = start & 127
        turn = (128 - inside) & 127
        views = [pltpu.roll(window(near_ref, tile + i, 0), turn, 1) for i in range(3)]
        kept = lane < 128 - inside
        first = jnp.where(kept, views[0], views[1])
        second = jnp.where(kept, views[1], views[2])
        start = start + 64
        tile = lax.shift_right_logical(start, 7)
        inside = start & 127
        turn = (128 - inside) & 127
        views = [pltpu.roll(window(far_ref, tile + i, 0), turn, 1) for i in range(2)]
        third = jnp.where(lane < 128 - inside, views[0], views[1])
        return jnp.where(line < 5, first, jnp.where(lane < 64, second, third))

    def band(a, most):
        for b in range(lons):
            one, two = pieces_of(limit_ref, a, b, lons)
            count = one[1] - one[0] - skipped
            shift = -float(TW * b) - COL_CODE
            value = take(one[0] + skipped)
            if two is None:
                value = value + jnp.where(col_line, shift, 0.0)
            else:
                total = float(TW * lons)
                first_shift, second_shift = (shift - total, shift) if b == 0 else (shift, shift + total)
                value = value + jnp.where(col_line, first_shift, 0.0)
                other = take(two[0] - count) + jnp.where(col_line, second_shift, 0.0)
                value = jnp.where(entry < count, value, other)
                count = count + two[1] - two[0]
            most = jnp.maximum(most, count)
            out_ref[a * lons + b] = jnp.where((entry < count) & ~meta, value, 0.0)
        return most

    most = lax.fori_loop(0, lats, band, 0)
    extra = jnp.maximum(most + (CAP - 1), 0) // CAP - 1
    extra = jnp.maximum(extra, 0).astype(f32)

    def flag(t, carry):
        out_ref[t, 7:8, 64:128] = jnp.full((1, 64), extra, f32)
        return carry

    lax.fori_loop(0, lats * lons, flag, 0)


def place(round_index, limits, keys, rows, fy, fx, values, lats, lons):
    vmem = pl.BlockSpec(memory_space=pltpu.VMEM)
    smem = pl.BlockSpec(memory_space=pltpu.SMEM)
    tiles = keys.shape[0] // 128
    columns = [x.reshape(tiles, 128) for x in (keys, rows, fy, fx, values)]
    scratch = pltpu.VMEM((8 * (tiles + 2 * PAD), 128), f32)
    return pl.pallas_call(
        functools.partial(place_kernel, lats=lats, lons=lons),
        out_shape=jax.ShapeDtypeStruct((lats * lons, 8, 128), f32),
        in_specs=[smem, smem] + [vmem] * 5,
        out_specs=vmem,
        scratch_shapes=[scratch, scratch],
        compiler_params=pltpu.CompilerParams(vmem_limit_bytes=16 * 1024 * 1024),
        name="place",
    )(round_index, limits, *columns)


def untouched(shape):
    return pl.pallas_call(
        lambda ref: None,
        out_shape=jax.ShapeDtypeStruct(shape, f32),
        out_specs=pl.BlockSpec(memory_space=pl.ANY),
        name="untouched",
    )()


def taper(distance, kappa):
    square = distance * distance
    inside = jnp.maximum(1.0 - square * (1.0 / (RAD * RAD)), 0.0)
    return jnp.exp2(square * (-LOG2E / kappa)) * (inside * inside)


def spread(window, group_of, groups):
    tiles = [window[16 * i : 16 * i + 16] for i in range(window.shape[0] // 16)]
    wide = jnp.broadcast_to(group_of, (16, 128))
    zero = jnp.zeros((16, 128), bf16)
    hits = [wide == float(g) for g in range(1 - len(tiles), groups)]
    out = []
    for g in range(groups):
        value = zero
        for i in range(len(tiles)):
            value = jnp.where(hits[g - i + len(tiles) - 1], tiles[i], value)
        out.append(value)
    return jnp.concatenate(out, axis=0)


def analyse_kernel(
    extra_count, arrived_ref, more_ref, mid_ref, north_ref, south_ref, out_ref,
    table, dep_ref, field_ref, lhs_ref, acc_ref, left_ref, window_ref, bounds, extra_ref, sem,
):
    sources = arrived_ref.shape[0]
    sources = sources // 8
    slot_line = lax.broadcasted_iota(jnp.int32, (CAP, sources), 0)

    def load_round(src, first):
        turned = [jnp.transpose(src[pl.ds(i, sources, stride=8), :]) for i in range(8)]
        for i in range(5):
            table[i, pl.ds(first, 128), :] = turned[i]
            half = 64 * (i % 2)
            table[i, pl.ds(first + 128, 64), :] = turned[5 + i // 2][half : half + 64]
        there = table[0, pl.ds(first, CAP), :] > 0.0
        return jnp.max(jnp.where(there, slot_line + 1, 0))

    used = load_round(arrived_ref, 0)
    extra = extra_count[0]

    def more_rounds(k, used):
        copy = pltpu.make_async_copy(more_ref.at[k], extra_ref, sem)
        copy.start()
        copy.wait()
        count = load_round(extra_ref, pl.multiple_of((k + 1) * CAP, 64))
        return jnp.where(count > 0, (k + 1) * CAP + count, used)

    used = lax.fori_loop(0, extra, more_rounds, used)
    chunks = (used + 7) // 8

    field_ref[0:MARGIN] = north_ref[...]
    field_ref[MARGIN : MARGIN + TH] = mid_ref[...]
    field_ref[MARGIN + TH :] = south_ref[...]

    def rows8(i, k):
        return table[i, pl.ds(pl.multiple_of(k * 8, 8), 8), :]

    def find_bounds(k, carry):
        there = rows8(0, k) > 0.0
        col = rows8(1, k) + (COL_CODE + MARGIN)
        bounds[0, k] = jnp.min(jnp.where(there, col, 511.0)).astype(jnp.int32)
        bounds[1, k] = jnp.max(jnp.where(there, col, 0.0)).astype(jnp.int32)
        return carry

    lax.fori_loop(0, chunks, find_bounds, 0)
    for i in range(5):
        table[i, pl.ds(pl.multiple_of(chunks * 8, 8), 8), :] = jnp.zeros((8, sources), f32)
    bounds[0, chunks] = 0
    bounds[1, chunks] = 0

    line8 = lax.broadcasted_iota(jnp.int32, (8, 128), 0).astype(f32)
    line256 = lax.broadcasted_iota(jnp.int32, (256, 128), 0).astype(f32).astype(bf16)
    ones = jnp.ones((256, 128), bf16)
    zeros = jnp.zeros((256, 128), bf16)
    line48 = lax.broadcasted_iota(jnp.int32, (48, 128), 0).astype(f32)

    def prepare(first_row, height):
        field = field_ref[first_row : first_row + height]
        beside = pltpu.roll(field, LANES - 1, 1)
        empty = jnp.zeros((height, 128), bf16)
        for part, grid in enumerate((field, beside)):
            high = grid.astype(bf16)
            low = (grid - high.astype(f32)).astype(bf16)
            rows = slice(part * height, (part + 1) * height)
            for i, split in enumerate((high, low)):
                for b in range(4):
                    piece = split[:, 128 * b : 128 * b + 128]
                    lhs_ref[b, rows, 256 * i : 256 * i + 128] = piece
                    if b > 0:
                        lhs_ref[b - 1, rows, 256 * i + 128 : 256 * i + 256] = piece
                lhs_ref[3, rows, 256 * i + 128 : 256 * i + 256] = empty

    def interpolate(k, block, first_row, height):
        groups = height // 8
        row = rows8(0, k) + (MARGIN - ROW_CODE - first_row)
        off = rows8(1, k) + (COL_CODE + MARGIN) - (block * 128).astype(f32)
        frac_row = rows8(2, k)
        frac_col = rows8(3, k)
        group = jnp.floor(row * 0.125)
        below = row - 8.0 * group
        hot = jnp.concatenate(
            [
                jnp.where(jnp.broadcast_to(off[j : j + 1].astype(bf16), (256, 128)) == line256, ones, zeros)
                for j in range(8)
            ],
            axis=1,
        )
        lines = jnp.dot(
            lhs_ref[block, 0 : 2 * height], jnp.concatenate([hot, hot], axis=0), preferred_element_type=f32
        )
        out = []
        for j in range(8):
            mine = lines[:, 128 * j : 128 * j + 128]
            which = jnp.broadcast_to(group[j : j + 1], (8, 128))
            picked = [jnp.zeros((8, 128), f32) for _ in range(4)]
            for g in range(groups):
                hit = which == float(g)
                for part in range(2):
                    first = part * height + 8 * g
                    picked[2 * part] = jnp.where(hit, mine[first : first + 8], picked[2 * part])
                    if g + 1 < groups:
                        picked[2 * part + 1] = jnp.where(hit, mine[first + 8 : first + 16], picked[2 * part + 1])
            fx = frac_col[j : j + 1]
            fy = frac_row[j : j + 1]
            near = line8 - jnp.broadcast_to(below[j : j + 1], (8, 128))
            weight_a = jnp.where(near == 0.0, 1.0 - fy, jnp.where(near == 1.0, fy, 0.0))
            weight_b = jnp.where(near == -7.0, fy, 0.0)
            mixed = weight_a * ((1.0 - fx) * picked[0] + fx * picked[2]) + weight_b * (
                (1.0 - fx) * picked[1] + fx * picked[3]
            )
            out.append(jnp.sum(mixed, axis=0, keepdims=True))
        return jnp.concatenate(out, axis=0)

    def at8(k):
        return pl.ds(pl.multiple_of(k * 8, 8), 8)

    def low_block(k):
        return lax.shift_right_logical(bounds[0, k], 7)

    def depart(k, first_row, height):
        dep_ref[at8(k), :] = rows8(4, k) - interpolate(k, low_block(k), first_row, height)

    def depart_rest(k, first_row, height):
        def pair(w, carry):
            block = low_block(k) + 2 * w
            dep_ref[at8(k), :] -= interpolate(k, block, first_row, height)
            return carry

        high_block = lax.shift_right_logical(bounds[1, k], 7)
        lax.fori_loop(1, lax.shift_right_logical(high_block - low_block(k), 1) + 1, pair, 0)

    def first_window(k):
        return lax.shift_right_logical(jnp.maximum(bounds[0, k] - (RAD - 1), 0), 7)

    def add_window(left, col_windows, col_group, block, height):
        shifted = col_group - (block * 8).astype(f32)
        right = jnp.concatenate(
            [spread(col_windows[j], shifted[j : j + 1].astype(bf16), 16) for j in range(8)], axis=1
        )
        both = lax.dot_general(left, right, (((1,), (1,)), ((), ())), preferred_element_type=f32)
        acc_ref[block, 0:height] += both[:, 0:128]
        acc_ref[block + 1, 0:height] += both[:, 128:256]

    def column_parts(k):
        col = rows8(1, k) + (COL_CODE + MARGIN)
        col_group = jnp.floor((col - (RAD - 1.0)) * 0.0625)
        return col_group, 16.0 * col_group - col

    def add_sums(k, kappa, row_shift, groups):
        dep = dep_ref[at8(k), :]
        row = rows8(0, k) + (row_shift - ROW_CODE)
        frac_row = rows8(2, k)
        frac_col = rows8(3, k)
        row_group = jnp.floor((row - (RAD - 1.0)) * 0.0625)
        row_from = 16.0 * row_group - row
        col_group, col_from = column_parts(k)
        left = []
        col_windows = []
        for j in range(8):
            gap = (line48 + row_from[j : j + 1]) - frac_row[j : j + 1]
            weight = taper(gap, kappa)
            which = row_group[j : j + 1].astype(bf16)
            numer = spread((weight * dep[j : j + 1]).astype(bf16), which, groups)
            denom = spread(weight.astype(bf16), which, groups)
            left.append(jnp.concatenate([numer, denom], axis=0))
            gap = (line48 + col_from[j : j + 1]) - frac_col[j : j + 1]
            col_windows.append(taper(gap, kappa).astype(bf16))
        left = jnp.concatenate(left, axis=1)
        height = 32 * groups
        left_ref[0:height] = left
        for j in range(8):
            window_ref[j] = col_windows[j]
        add_window(left, col_windows, col_group, first_window(k), height)

    def add_rest(k, groups):
        height = 32 * groups

        def pair(w, carry):
            col_group = column_parts(k)[0]
            windows = [window_ref[j] for j in range(8)]
            add_window(left_ref[0:height], windows, col_group, first_window(k) + 2 * w, height)
            return carry

        last = lax.shift_right_logical(jnp.minimum(bounds[1, k] + RAD, LANES - 1), 7)
        lax.fori_loop(1, lax.shift_right_logical(last - first_window(k), 1) + 1, pair, 0)

    def one_pass(kappa, first_row, field_height, row_shift, groups):
        prepare(first_row, field_height)
        acc_ref[...] = jnp.zeros_like(acc_ref)

        def ahead(k, carry):
            depart(k, first_row, field_height)
            depart_rest(k, first_row, field_height)
            return carry

        lax.fori_loop(0, jnp.minimum(chunks, 1), ahead, 0)

        def chunk(k, carry):
            following = jnp.minimum(k + 1, chunks)
            add_sums(k, kappa, row_shift, groups)
            depart(following, first_row, field_height)
            add_rest(k, groups)
            depart_rest(following, first_row, field_height)
            return carry

        lax.fori_loop(0, chunks, chunk, 0)

    one_pass(KAPPA_ONE, 0, EXT_ROWS, 16.0, 10)
    field_ref[0:8] = jnp.zeros((8, LANES), f32)
    field_ref[168:EXT_ROWS] = jnp.zeros((8, LANES), f32)
    for b in range(4):
        lanes = slice(128 * b, 128 * b + 128)
        field_ref[8:168, lanes] += acc_ref[b, 0:160] / (acc_ref[b, 160:320] + 1.0)
    one_pass(KAPPA_TWO, 8, 160, 0.0, 8)
    final = jnp.concatenate(
        [
            field_ref[MARGIN : MARGIN + TH, 128 * b : 128 * b + 128]
            + acc_ref[b, 0:TH] / (acc_ref[b, TH : 2 * TH] + 1.0)
            for b in range(4)
        ],
        axis=1,
    )
    out_ref[...] = pltpu.roll(final, LANES - MARGIN, 1)[:, 0:TW]


def analyse(extra, arrived, more, middle, north, south):
    vmem = pl.BlockSpec(memory_space=pltpu.VMEM)
    sources = arrived.shape[0]
    slots = ROUNDS * CAP
    return pl.pallas_call(
        analyse_kernel,
        out_shape=jax.ShapeDtypeStruct((TH, TW), f32),
        in_specs=[pl.BlockSpec(memory_space=pltpu.SMEM), vmem, pl.BlockSpec(memory_space=pl.ANY), vmem, vmem, vmem],
        out_specs=vmem,
        scratch_shapes=[
            pltpu.VMEM((5, slots + 8, sources), f32),
            pltpu.VMEM((slots + 8, sources), f32),
            pltpu.VMEM((EXT_ROWS, LANES), f32),
            pltpu.VMEM((4, 2 * EXT_ROWS, 512), bf16),
            pltpu.VMEM((5, 320, 128), f32),
            pltpu.VMEM((320, 8 * sources), bf16),
            pltpu.VMEM((8, 48, sources), bf16),
            pltpu.SMEM((2, slots // 8 + 1), jnp.int32),
            pltpu.VMEM((sources * 8, 128), f32),
            pltpu.SemaphoreType.DMA,
        ],
        compiler_params=pltpu.CompilerParams(vmem_limit_bytes=48 * 1024 * 1024),
        name="analyse",
    )(extra.reshape(1), arrived.reshape(sources * 8, 128), more, middle, north, south)


def on_device(background, obs_cell, obs_frac, obs_value):
    lats = lax.axis_size("lat")
    lons = lax.axis_size("lon")
    axes = ("lat", "lon")
    devices = lats * lons

    west = neighbour(background[:, TW - MARGIN :], "lon", 1, True)
    east = neighbour(background[:, :MARGIN], "lon", -1, True)
    spare = jnp.zeros((TH, LANES - TW - 2 * MARGIN), f32)
    middle = jnp.concatenate([west, background, east, spare], axis=1)
    north = neighbour(middle[TH - MARGIN :], "lat", 1, False)
    south = neighbour(middle[:MARGIN], "lat", -1, False)

    columns = sort_observations(obs_cell, obs_frac, obs_value, lats)
    limits = segment_limits(columns[0], lats, lons)

    def exchange(k):
        outgoing = place(k.reshape(1), limits, *columns, lats, lons)
        return lax.all_to_all(outgoing, axes, split_axis=0, concat_axis=0, tiled=True)

    arrived = exchange(jnp.int32(0))
    extra = jnp.max(arrived[:, 7, 127]).astype(jnp.int32)

    def one_more(k, held):
        got = exchange(k + 1).reshape(1, devices * 8, 128)
        return lax.dynamic_update_slice_in_dim(held, got, k, 0)

    more = lax.fori_loop(0, extra, one_more, untouched((ROUNDS - 1, devices * 8, 128)))
    return analyse(extra, arrived, more, middle, north, south)


def solution(mesh):
    placed = (P("lat", "lon"), P(None, ("lat", "lon")), P(None, ("lat", "lon")), P(("lat", "lon")))
    return jax.shard_map(
        on_device, mesh=mesh, in_specs=placed, out_specs=P("lat", "lon"), check_vma=False
    )
```

```python
import functools

import jax
import jax.numpy as jnp
from jax import lax
from jax.experimental import pallas as pl
from jax.experimental.pallas import tpu as pltpu
from jax.sharding import PartitionSpec as P

RAD = 12
MARGIN = 24
TH = 128
TW = 384
CAP = 192
ROUNDS = 6
BAND = 8192
NOWHERE = 1 << 30
PAD = 4
EXT_ROWS = TH + 2 * MARGIN
LANES = 512
ROW_CODE = 64.0
COL_CODE = 192.0
LOG2E = 1.4426950408889634
KAPPA_ONE = RAD * RAD / 9.0
KAPPA_TWO = 0.35 * KAPPA_ONE
f32 = jnp.float32
bf16 = jnp.bfloat16


def neighbour(block, axis, distance, wrap):
    count = lax.axis_size(axis)
    route = [(i, (i + distance) % count) for i in range(count) if wrap or 0 <= i + distance < count]
    return lax.ppermute(block, axis, route)


def key_kernel(cell_ref, frac_ref, value_ref, key_ref, rows_ref, fy_ref, fx_ref, out_ref, row_ref, col_ref, *, lats):
    half = row_ref.shape[0]
    for i in range(half):
        lanes = slice(128 * i, 128 * i + 128)
        line = slice(i, i + 1)
        row_ref[line] = cell_ref[0:1, lanes]
        col_ref[line] = cell_ref[1:2, lanes]
        fy_ref[line] = frac_ref[0:1, lanes]
        fx_ref[line] = frac_ref[1:2, lanes]
        out_ref[line] = value_ref[0:1, lanes]
    for ref in (fy_ref, fx_ref, out_ref):
        ref[half : 2 * half] = ref[0:half]
    row = row_ref[...]
    lat = lax.shift_right_logical(row, 7)
    local_row = row - lat * TH
    up = (local_row <= MARGIN - 2) & (lat > 0)
    down = (local_row >= TH - MARGIN) & (lat < lats - 1)
    move = jnp.where(up, -1, jnp.where(down, 1, 0))
    own_key = lat * BAND + col_ref[...]
    key_ref[0:half] = own_key
    key_ref[half : 2 * half] = jnp.where(move == 0, NOWHERE, own_key + move * BAND)
    rows_ref[0:half] = local_row.astype(f32) + ROW_CODE
    rows_ref[half : 2 * half] = (local_row - move * TH).astype(f32) + ROW_CODE


def sort_observations(obs_cell, obs_frac, obs_value, lats):
    vmem = pl.BlockSpec(memory_space=pltpu.VMEM)
    half = obs_value.shape[0] // 128
    whole = jax.ShapeDtypeStruct((2 * half, 128), f32)
    scratch = pltpu.VMEM((half, 128), jnp.int32)
    columns = pl.pallas_call(
        functools.partial(key_kernel, lats=lats),
        out_shape=[jax.ShapeDtypeStruct((2 * half, 128), jnp.int32)] + [whole] * 4,
        in_specs=[vmem] * 3,
        out_specs=[vmem] * 5,
        scratch_shapes=[scratch, scratch],
        name="keys",
    )(obs_cell, obs_frac, obs_value[None, :])
    return lax.sort([x.reshape(256 * half) for x in columns], num_keys=1, is_stable=False)


def segment_limits(keys, lats, lons):
    low = [TW * b - MARGIN for b in range(lons)]
    high = [TW * (b + 1) + MARGIN - 1 for b in range(lons)]
    total = TW * lons
    band = low + high + [0, total]
    band[0] += total
    band[2 * lons - 1] -= total
    limits = jnp.array([a * BAND + x for a in range(lats) for x in band], jnp.int32)
    return jnp.sum((keys[None, :] < limits[:, None]).astype(jnp.int32), axis=1)


def pieces_of(limit_ref, a, b, lons):
    base = a * (2 * lons + 2)
    first = limit_ref[base + b]
    end = limit_ref[base + lons + b]
    if b == 0:
        return (first, limit_ref[base + 2 * lons + 1]), (limit_ref[base + 2 * lons], end)
    if b == lons - 1:
        return (first, limit_ref[base + 2 * lons + 1]), (limit_ref[base + 2 * lons], end)
    return (first, end), None


def place_kernel(round_ref, limit_ref, key_ref, row_ref, fy_ref, fx_ref, value_ref, out_ref, near_ref, far_ref, *, lats, lons):
    tiles = key_ref.shape[0]
    skipped = round_ref[0] * CAP
    col = (key_ref[...] & (BAND - 1)).astype(f32)
    near = [row_ref[...], col, fy_ref[...], fx_ref[...], value_ref[...], row_ref[...], fy_ref[...], value_ref[...]]
    lane = lax.broadcasted_iota(jnp.int32, (8, 128), 1)
    line = lax.broadcasted_iota(jnp.int32, (8, 128), 0)
    for i, x in enumerate(near):
        near_ref[pl.ds(8 * PAD + i, tiles, stride=8), :] = x
    for i, x in ((5, col), (6, fx_ref[...])):
        far_ref[pl.ds(8 * PAD + i, tiles, stride=8), :] = x
    entry = jnp.where(line < 5, lane, 128 + (lane & 63))
    col_line = (line == 1) | ((line == 5) & (lane >= 64))
    meta = (line == 7) & (lane >= 64)

    def window(ref, tile, start):
        return ref[pl.ds(pl.multiple_of(tile * 8, 8), 8), :]

    def take(start):
        start = jnp.clip(start + 128 * PAD, 0, (tiles + PAD) * 128)
        tile = lax.shift_right_logical(start, 7)
        inside = start & 127
        turn = (128 - inside) & 127
        views = [pltpu.roll(window(near_ref, tile + i, 0), turn, 1) for i in range(3)]
        kept = lane < 128 - inside
        first = jnp.where(kept, views[0], views[1])
        second = jnp.where(kept, views[1], views[2])
        start = start + 64
        tile = lax.shift_right_logical(start, 7)
        inside = start & 127
        turn = (128 - inside) & 127
        views = [pltpu.roll(window(far_ref, tile + i, 0), turn, 1) for i in range(2)]
        third = jnp.where(lane < 128 - inside, views[0], views[1])
        return jnp.where(line < 5, first, jnp.where(lane < 64, second, third))

    def band(a, most):
        for b in range(lons):
            one, two = pieces_of(limit_ref, a, b, lons)
            count = one[1] - one[0] - skipped
            shift = -float(TW * b) - COL_CODE
            value = take(one[0] + skipped)
            if two is None:
                value = value + jnp.where(col_line, shift, 0.0)
            else:
                total = float(TW * lons)
                first_shift, second_shift = (shift - total, shift) if b == 0 else (shift, shift + total)
                value = value + jnp.where(col_line, first_shift, 0.0)
                other = take(two[0] - count) + jnp.where(col_line, second_shift, 0.0)
                value = jnp.where(entry < count, value, other)
                count = count + two[1] - two[0]
            most = jnp.maximum(most, count)
            out_ref[a * lons + b] = jnp.where((entry < count) & ~meta, value, 0.0)
        return most

    most = lax.fori_loop(0, lats, band, 0)
    extra = jnp.maximum(most + (CAP - 1), 0) // CAP - 1
    extra = jnp.maximum(extra, 0).astype(f32)

    def flag(t, carry):
        out_ref[t, 7:8, 64:128] = jnp.full((1, 64), extra, f32)
        return carry

    lax.fori_loop(0, lats * lons, flag, 0)


def place(round_index, limits, keys, rows, fy, fx, values, lats, lons):
    vmem = pl.BlockSpec(memory_space=pltpu.VMEM)
    smem = pl.BlockSpec(memory_space=pltpu.SMEM)
    tiles = keys.shape[0] // 128
    columns = [x.reshape(tiles, 128) for x in (keys, rows, fy, fx, values)]
    scratch = pltpu.VMEM((8 * (tiles + 2 * PAD), 128), f32)
    return pl.pallas_call(
        functools.partial(place_kernel, lats=lats, lons=lons),
        out_shape=jax.ShapeDtypeStruct((lats * lons, 8, 128), f32),
        in_specs=[smem, smem] + [vmem] * 5,
        out_specs=vmem,
        scratch_shapes=[scratch, scratch],
        compiler_params=pltpu.CompilerParams(vmem_limit_bytes=16 * 1024 * 1024),
        cost_estimate=pl.CostEstimate(flops=4_000_000_000, bytes_accessed=4_000_000, transcendentals=0),
        name="place",
    )(round_index, limits, *columns)


def untouched(shape):
    return pl.pallas_call(
        lambda ref: None,
        out_shape=jax.ShapeDtypeStruct(shape, f32),
        out_specs=pl.BlockSpec(memory_space=pl.ANY),
        name="untouched",
    )()


def taper(distance, kappa):
    square = distance * distance
    inside = jnp.maximum(1.0 - square * (1.0 / (RAD * RAD)), 0.0)
    return jnp.exp2(square * (-LOG2E / kappa)) * (inside * inside)


def spread(window, group_of, groups):
    tiles = [window[16 * i : 16 * i + 16] for i in range(window.shape[0] // 16)]
    wide = jnp.broadcast_to(group_of, (16, 128))
    zero = jnp.zeros((16, 128), bf16)
    hits = [wide == float(g) for g in range(1 - len(tiles), groups)]
    out = []
    for g in range(groups):
        value = zero
        for i in range(len(tiles)):
            value = jnp.where(hits[g - i + len(tiles) - 1], tiles[i], value)
        out.append(value)
    return jnp.concatenate(out, axis=0)


def analyse_kernel(
    extra_count, arrived_ref, more_ref, mid_ref, north_ref, south_ref, out_ref,
    table, dep_ref, field_ref, lhs_ref, acc_ref, left_ref, window_ref, bounds, extra_ref, sem,
):
    sources = arrived_ref.shape[0]
    sources = sources // 8
    slot_line = lax.broadcasted_iota(jnp.int32, (CAP, sources), 0)

    def load_round(src, first):
        turned = [jnp.transpose(src[pl.ds(i, sources, stride=8), :]) for i in range(8)]
        for i in range(5):
            table[i, pl.ds(first, 128), :] = turned[i]
            half = 64 * (i % 2)
            table[i, pl.ds(first + 128, 64), :] = turned[5 + i // 2][half : half + 64]
        there = table[0, pl.ds(first, CAP), :] > 0.0
        return jnp.max(jnp.where(there, slot_line + 1, 0))

    used = load_round(arrived_ref, 0)
    extra = extra_count[0]

    def more_rounds(k, used):
        copy = pltpu.make_async_copy(more_ref.at[k], extra_ref, sem)
        copy.start()
        copy.wait()
        count = load_round(extra_ref, pl.multiple_of((k + 1) * CAP, 64))
        return jnp.where(count > 0, (k + 1) * CAP + count, used)

    used = lax.fori_loop(0, extra, more_rounds, used)
    chunks = (used + 7) // 8

    field_ref[0:MARGIN] = north_ref[...]
    field_ref[MARGIN : MARGIN + TH] = mid_ref[...]
    field_ref[MARGIN + TH :] = south_ref[...]

    def rows8(i, k):
        return table[i, pl.ds(pl.multiple_of(k * 8, 8), 8), :]

    def find_bounds(k, carry):
        there = rows8(0, k) > 0.0
        col = rows8(1, k) + (COL_CODE + MARGIN)
        bounds[0, k] = jnp.min(jnp.where(there, col, 511.0)).astype(jnp.int32)
        bounds[1, k] = jnp.max(jnp.where(there, col, 0.0)).astype(jnp.int32)
        return carry

    lax.fori_loop(0, chunks, find_bounds, 0)
    for i in range(5):
        table[i, pl.ds(pl.multiple_of(chunks * 8, 8), 8), :] = jnp.zeros((8, sources), f32)
    bounds[0, chunks] = 0
    bounds[1, chunks] = 0

    line8 = lax.broadcasted_iota(jnp.int32, (8, 128), 0).astype(f32)
    line256 = lax.broadcasted_iota(jnp.int32, (256, 128), 0).astype(f32).astype(bf16)
    zeros = jnp.zeros((256, 128), bf16)
    line32 = lax.broadcasted_iota(jnp.int32, (32, 128), 0).astype(f32)
    empty8 = jnp.zeros((8, 128), f32)

    def aligned(window, late):
        late = jnp.broadcast_to(late, (8, 128)) > 0.0
        tiles = [empty8] + [window[8 * i : 8 * i + 8] for i in range(4)] + [empty8]
        moved = [jnp.where(late, tiles[i], tiles[i + 1]) for i in range(5)] + [empty8]
        return jnp.concatenate(moved, axis=0).astype(bf16)

    def start_of(position):
        eighth = jnp.floor((position - (RAD - 1.0)) * 0.125)
        group = jnp.floor(eighth * 0.5)
        return group, eighth - 2.0 * group, 8.0 * eighth - position

    def prepare(first_row, height):
        field = field_ref[first_row : first_row + height]
        high = field.astype(bf16)
        low = (field - high.astype(f32)).astype(bf16)
        empty = jnp.zeros((height, 128), bf16)
        for i, split in enumerate((high, low, high)):
            for b in range(4):
                piece = split[:, 128 * b : 128 * b + 128]
                lhs_ref[b, 0:height, 256 * i : 256 * i + 128] = piece
                if b > 0:
                    lhs_ref[b - 1, 0:height, 256 * i + 128 : 256 * i + 256] = piece
            lhs_ref[3, 0:height, 256 * i + 128 : 256 * i + 256] = empty

    def both_parts(x):
        high = x.astype(bf16)
        return high, (x - high.astype(f32)).astype(bf16)

    def interpolate(k, block, first_row, height):
        groups = height // 8
        row = rows8(0, k) + (MARGIN - ROW_CODE - first_row)
        off = rows8(1, k) + (COL_CODE + MARGIN) - (block * 128).astype(f32)
        frac_row = rows8(2, k)
        frac_col = rows8(3, k)
        group = jnp.floor(row * 0.125)
        below = row - 8.0 * group
        here, after = both_parts(1.0 - frac_col), both_parts(frac_col)
        next_off = (off + 1.0).astype(bf16)
        off = off.astype(bf16)
        mixes = ([], [])
        for j in range(8):
            one = slice(j, j + 1)
            at_col = jnp.broadcast_to(off[one], (256, 128)) == line256
            at_next = jnp.broadcast_to(next_off[one], (256, 128)) == line256
            for part in range(2):
                mixes[part].append(
                    jnp.where(
                        at_col,
                        jnp.broadcast_to(here[part][one], (256, 128)),
                        jnp.where(at_next, jnp.broadcast_to(after[part][one], (256, 128)), zeros),
                    )
                )
        high = jnp.concatenate(mixes[0], axis=1)
        low = jnp.concatenate(mixes[1], axis=1)
        lines = jnp.dot(
            lhs_ref[block, 0:height],
            jnp.concatenate([high, high, low], axis=0),
            preferred_element_type=f32,
        )
        out = []
        for j in range(8):
            mine = lines[:, 128 * j : 128 * j + 128]
            which = jnp.broadcast_to(group[j : j + 1], (8, 128))
            same = jnp.zeros((8, 128), f32)
            following = jnp.zeros((8, 128), f32)
            for g in range(groups):
                hit = which == float(g)
                same = jnp.where(hit, mine[8 * g : 8 * g + 8], same)
                if g + 1 < groups:
                    following = jnp.where(hit, mine[8 * g + 8 : 8 * g + 16], following)
            fy = frac_row[j : j + 1]
            near = line8 - jnp.broadcast_to(below[j : j + 1], (8, 128))
            weight_a = jnp.where(near == 0.0, 1.0 - fy, jnp.where(near == 1.0, fy, 0.0))
            weight_b = jnp.where(near == -7.0, fy, 0.0)
            out.append(jnp.sum(weight_a * same + weight_b * following, axis=0, keepdims=True))
        return jnp.concatenate(out, axis=0)

    def at8(k):
        return pl.ds(pl.multiple_of(k * 8, 8), 8)

    def low_block(k):
        return lax.shift_right_logical(bounds[0, k], 7)

    def depart(k, first_row, height):
        dep_ref[at8(k), :] = rows8(4, k) - interpolate(k, low_block(k), first_row, height)

    def depart_rest(k, first_row, height):
        def pair(w, carry):
            block = low_block(k) + 2 * w
            dep_ref[at8(k), :] -= interpolate(k, block, first_row, height)
            return carry

        high_block = lax.shift_right_logical(bounds[1, k] + 1, 7)
        lax.fori_loop(1, lax.shift_right_logical(high_block - low_block(k), 1) + 1, pair, 0)

    def first_window(k):
        return lax.shift_right_logical(jnp.maximum(bounds[0, k] - (RAD - 1), 0), 7)

    def add_window(left, col_windows, col_group, block, height):
        shifted = col_group - (block * 8).astype(f32)
        right = jnp.concatenate(
            [spread(col_windows[j], shifted[j : j + 1].astype(bf16), 16) for j in range(8)], axis=1
        )
        both = lax.dot_general(left, right, (((1,), (1,)), ((), ())), preferred_element_type=f32)
        acc_ref[block, 0:height] += both[:, 0:128]
        acc_ref[block + 1, 0:height] += both[:, 128:256]

    def column_parts(k):
        col = rows8(1, k) + (COL_CODE + MARGIN)
        return start_of(col)

    def add_sums(k, kappa, row_shift, groups):
        dep = dep_ref[at8(k), :]
        row = rows8(0, k) + (row_shift - ROW_CODE)
        frac_row = rows8(2, k)
        frac_col = rows8(3, k)
        row_group, row_late, row_from = start_of(row)
        col_group, col_late, col_from = column_parts(k)
        left = []
        col_windows = []
        for j in range(8):
            gap = (line32 + row_from[j : j + 1]) - frac_row[j : j + 1]
            weight = taper(gap, kappa)
            which = row_group[j : j + 1].astype(bf16)
            late = row_late[j : j + 1]
            numer = spread(aligned(weight * dep[j : j + 1], late), which, groups)
            denom = spread(aligned(weight, late), which, groups)
            left.append(jnp.concatenate([numer, denom], axis=0))
            gap = (line32 + col_from[j : j + 1]) - frac_col[j : j + 1]
            col_windows.append(aligned(taper(gap, kappa), col_late[j : j + 1]))
        left = jnp.concatenate(left, axis=1)
        height = 32 * groups
        left_ref[0:height] = left
        for j in range(8):
            window_ref[j] = col_windows[j]
        add_window(left_ref[0:height], col_windows, col_group, first_window(k), height)

    def add_rest(k, groups):
        height = 32 * groups

        def pair(w, carry):
            col_group = column_parts(k)[0]
            windows = [window_ref[j] for j in range(8)]
            add_window(left_ref[0:height], windows, col_group, first_window(k) + 2 * w, height)
            return carry

        last = lax.shift_right_logical(jnp.minimum(bounds[1, k] + RAD, LANES - 1), 7)
        lax.fori_loop(1, lax.shift_right_logical(last - first_window(k), 1) + 1, pair, 0)

    def one_pass(kappa, first_row, field_height, row_shift, groups):
        prepare(first_row, field_height)
        acc_ref[...] = jnp.zeros_like(acc_ref)

        def ahead(k, carry):
            depart(k, first_row, field_height)
            depart_rest(k, first_row, field_height)
            return carry

        lax.fori_loop(0, jnp.minimum(chunks, 1), ahead, 0)

        def chunk(k, carry):
            following = jnp.minimum(k + 1, chunks)
            add_sums(k, kappa, row_shift, groups)
            depart(following, first_row, field_height)
            add_rest(k, groups)
            depart_rest(following, first_row, field_height)
            return carry

        lax.fori_loop(0, chunks, chunk, 0)

    one_pass(KAPPA_ONE, 0, EXT_ROWS, 16.0, 10)
    field_ref[0:8] = jnp.zeros((8, LANES), f32)
    field_ref[168:EXT_ROWS] = jnp.zeros((8, LANES), f32)
    for b in range(4):
        lanes = slice(128 * b, 128 * b + 128)
        field_ref[8:168, lanes] += acc_ref[b, 0:160] / (acc_ref[b, 160:320] + 1.0)
    one_pass(KAPPA_TWO, 8, 160, 0.0, 8)
    final = jnp.concatenate(
        [
            field_ref[MARGIN : MARGIN + TH, 128 * b : 128 * b + 128]
            + acc_ref[b, 0:TH] / (acc_ref[b, TH : 2 * TH] + 1.0)
            for b in range(4)
        ],
        axis=1,
    )
    out_ref[...] = pltpu.roll(final, LANES - MARGIN, 1)[:, 0:TW]


def analyse(extra, arrived, more, middle, north, south):
    vmem = pl.BlockSpec(memory_space=pltpu.VMEM)
    sources = arrived.shape[0]
    slots = ROUNDS * CAP
    return pl.pallas_call(
        analyse_kernel,
        out_shape=jax.ShapeDtypeStruct((TH, TW), f32),
        in_specs=[pl.BlockSpec(memory_space=pltpu.SMEM), vmem, pl.BlockSpec(memory_space=pl.ANY), vmem, vmem, vmem],
        out_specs=vmem,
        scratch_shapes=[
            pltpu.VMEM((5, slots + 8, sources), f32),
            pltpu.VMEM((slots + 8, sources), f32),
            pltpu.VMEM((EXT_ROWS, LANES), f32),
            pltpu.VMEM((4, EXT_ROWS, 768), bf16),
            pltpu.VMEM((5, 320, 128), f32),
            pltpu.VMEM((320, 8 * sources), bf16),
            pltpu.VMEM((8, 48, sources), bf16),
            pltpu.SMEM((2, slots // 8 + 1), jnp.int32),
            pltpu.VMEM((sources * 8, 128), f32),
            pltpu.SemaphoreType.DMA,
        ],
        compiler_params=pltpu.CompilerParams(vmem_limit_bytes=48 * 1024 * 1024),
        name="analyse",
    )(extra.reshape(1), arrived.reshape(sources * 8, 128), more, middle, north, south)


def on_device(background, obs_cell, obs_frac, obs_value):
    lats = lax.axis_size("lat")
    lons = lax.axis_size("lon")
    axes = ("lat", "lon")
    devices = lats * lons

    west = neighbour(background[:, TW - 128 :], "lon", 1, True)[:, 128 - MARGIN :]
    east = neighbour(background[:, :128], "lon", -1, True)[:, :MARGIN]
    spare = jnp.zeros((TH, LANES - TW - 2 * MARGIN), f32)
    middle = jnp.concatenate([west, background, east, spare], axis=1)

    columns = sort_observations(obs_cell, obs_frac, obs_value, lats)
    columns, middle = lax.optimization_barrier((columns, middle))
    limits = segment_limits(columns[0], lats, lons)

    def outgoing(k):
        return place(k.reshape(1), limits, *columns, lats, lons)

    def exchange(block):
        return lax.all_to_all(block, axes, split_axis=0, concat_axis=0, tiled=True)

    first, middle = lax.optimization_barrier((outgoing(jnp.int32(0)), middle))
    arrived = exchange(first)
    north = neighbour(middle[TH - MARGIN :], "lat", 1, False)
    south = neighbour(middle[:MARGIN], "lat", -1, False)
    extra = jnp.max(arrived[:, 7, 127]).astype(jnp.int32)

    def one_more(k, held):
        got = exchange(outgoing(k + 1)).reshape(1, devices * 8, 128)
        return lax.dynamic_update_slice_in_dim(held, got, k, 0)

    more = lax.fori_loop(0, extra, one_more, untouched((ROUNDS - 1, devices * 8, 128)))
    return analyse(extra, arrived, more, middle, north, south)


def solution(mesh):
    placed = (P("lat", "lon"), P(None, ("lat", "lon")), P(None, ("lat", "lon")), P(("lat", "lon")))
    return jax.shard_map(
        on_device, mesh=mesh, in_specs=placed, out_specs=P("lat", "lon"), check_vma=False
    )
```

```python
import functools

import jax
import jax.numpy as jnp
from jax import lax
from jax.experimental import pallas as pl
from jax.experimental.pallas import tpu as pltpu
from jax.sharding import PartitionSpec as P

RAD = 12
MARGIN = 24
TH = 128
TW = 384
CAP = 192
ROUNDS = 6
BAND = 8192
NOWHERE = 1 << 30
PAD = 4
EXT_ROWS = TH + 2 * MARGIN
LANES = 512
ROW_CODE = 64.0
COL_CODE = 192.0
LOG2E = 1.4426950408889634
KAPPA_ONE = RAD * RAD / 9.0
KAPPA_TWO = 0.35 * KAPPA_ONE
f32 = jnp.float32
bf16 = jnp.bfloat16


def neighbour(block, axis, distance, wrap):
    count = lax.axis_size(axis)
    route = [(i, (i + distance) % count) for i in range(count) if wrap or 0 <= i + distance < count]
    return lax.ppermute(block, axis, route)


def key_kernel(cell_ref, frac_ref, value_ref, key_ref, rows_ref, fy_ref, fx_ref, out_ref, row_ref, col_ref, *, lats):
    half = row_ref.shape[0]
    for i in range(half):
        lanes = slice(128 * i, 128 * i + 128)
        line = slice(i, i + 1)
        row_ref[line] = cell_ref[0:1, lanes]
        col_ref[line] = cell_ref[1:2, lanes]
        fy_ref[line] = frac_ref[0:1, lanes]
        fx_ref[line] = frac_ref[1:2, lanes]
        out_ref[line] = value_ref[0:1, lanes]
    for ref in (fy_ref, fx_ref, out_ref):
        ref[half : 2 * half] = ref[0:half]
    row = row_ref[...]
    lat = lax.shift_right_logical(row, 7)
    local_row = row - lat * TH
    up = (local_row <= MARGIN - 2) & (lat > 0)
    down = (local_row >= TH - MARGIN) & (lat < lats - 1)
    move = jnp.where(up, -1, jnp.where(down, 1, 0))
    own_key = lat * BAND + col_ref[...]
    key_ref[0:half] = own_key
    key_ref[half : 2 * half] = jnp.where(move == 0, NOWHERE, own_key + move * BAND)
    rows_ref[0:half] = local_row.astype(f32) + ROW_CODE
    rows_ref[half : 2 * half] = (local_row - move * TH).astype(f32) + ROW_CODE


def sort_observations(obs_cell, obs_frac, obs_value, lats):
    vmem = pl.BlockSpec(memory_space=pltpu.VMEM)
    half = obs_value.shape[0] // 128
    whole = jax.ShapeDtypeStruct((2 * half, 128), f32)
    scratch = pltpu.VMEM((half, 128), jnp.int32)
    columns = pl.pallas_call(
        functools.partial(key_kernel, lats=lats),
        out_shape=[jax.ShapeDtypeStruct((2 * half, 128), jnp.int32)] + [whole] * 4,
        in_specs=[vmem] * 3,
        out_specs=[vmem] * 5,
        scratch_shapes=[scratch, scratch],
        name="keys",
    )(obs_cell, obs_frac, obs_value[None, :])
    return lax.sort([x.reshape(256 * half) for x in columns], num_keys=1, is_stable=False)


def segment_limits(keys, lats, lons):
    low = [TW * b - MARGIN for b in range(lons)]
    high = [TW * (b + 1) + MARGIN - 1 for b in range(lons)]
    total = TW * lons
    band = low + high + [0, total]
    band[0] += total
    band[2 * lons - 1] -= total
    limits = jnp.array([a * BAND + x for a in range(lats) for x in band], jnp.int32)
    return jnp.sum((keys[None, :] < limits[:, None]).astype(jnp.int32), axis=1)


def pieces_of(limit_ref, a, b, lons):
    base = a * (2 * lons + 2)
    first = limit_ref[base + b]
    end = limit_ref[base + lons + b]
    if b == 0:
        return (first, limit_ref[base + 2 * lons + 1]), (limit_ref[base + 2 * lons], end)
    if b == lons - 1:
        return (first, limit_ref[base + 2 * lons + 1]), (limit_ref[base + 2 * lons], end)
    return (first, end), None


def place_kernel(round_ref, limit_ref, key_ref, row_ref, fy_ref, fx_ref, value_ref, out_ref, near_ref, far_ref, *, lats, lons):
    tiles = key_ref.shape[0]
    skipped = round_ref[0] * CAP
    col = (key_ref[...] & (BAND - 1)).astype(f32)
    near = [row_ref[...], col, fy_ref[...], fx_ref[...], value_ref[...], row_ref[...], fy_ref[...], value_ref[...]]
    lane = lax.broadcasted_iota(jnp.int32, (8, 128), 1)
    line = lax.broadcasted_iota(jnp.int32, (8, 128), 0)
    for i, x in enumerate(near):
        near_ref[pl.ds(8 * PAD + i, tiles, stride=8), :] = x
    for i, x in ((5, col), (6, fx_ref[...])):
        far_ref[pl.ds(8 * PAD + i, tiles, stride=8), :] = x
    entry = jnp.where(line < 5, lane, 128 + (lane & 63))
    col_line = (line == 1) | ((line == 5) & (lane >= 64))
    meta = (line == 7) & (lane >= 64)

    def window(ref, tile, start):
        return ref[pl.ds(pl.multiple_of(tile * 8, 8), 8), :]

    def take(start):
        start = jnp.clip(start + 128 * PAD, 0, (tiles + PAD) * 128)
        tile = lax.shift_right_logical(start, 7)
        inside = start & 127
        turn = (128 - inside) & 127
        views = [pltpu.roll(window(near_ref, tile + i, 0), turn, 1) for i in range(3)]
        kept = lane < 128 - inside
        first = jnp.where(kept, views[0], views[1])
        second = jnp.where(kept, views[1], views[2])
        start = start + 64
        tile = lax.shift_right_logical(start, 7)
        inside = start & 127
        turn = (128 - inside) & 127
        views = [pltpu.roll(window(far_ref, tile + i, 0), turn, 1) for i in range(2)]
        third = jnp.where(lane < 128 - inside, views[0], views[1])
        return jnp.where(line < 5, first, jnp.where(lane < 64, second, third))

    def band(a, most):
        for b in range(lons):
            one, two = pieces_of(limit_ref, a, b, lons)
            count = one[1] - one[0] - skipped
            shift = -float(TW * b) - COL_CODE
            value = take(one[0] + skipped)
            if two is None:
                value = value + jnp.where(col_line, shift, 0.0)
            else:
                total = float(TW * lons)
                first_shift, second_shift = (shift - total, shift) if b == 0 else (shift, shift + total)
                value = value + jnp.where(col_line, first_shift, 0.0)
                other = take(two[0] - count) + jnp.where(col_line, second_shift, 0.0)
                value = jnp.where(entry < count, value, other)
                count = count + two[1] - two[0]
            most = jnp.maximum(most, count)
            out_ref[a * lons + b] = jnp.where((entry < count) & ~meta, value, 0.0)
        return most

    most = lax.fori_loop(0, lats, band, 0)
    extra = jnp.maximum(most + (CAP - 1), 0) // CAP - 1
    extra = jnp.maximum(extra, 0).astype(f32)

    flags = jnp.full((1, 64), extra, f32)
    for t in range(lats * lons):
        out_ref[t, 7:8, 64:128] = flags


def place(round_index, limits, keys, rows, fy, fx, values, lats, lons):
    vmem = pl.BlockSpec(memory_space=pltpu.VMEM)
    smem = pl.BlockSpec(memory_space=pltpu.SMEM)
    tiles = keys.shape[0] // 128
    columns = [x.reshape(tiles, 128) for x in (keys, rows, fy, fx, values)]
    scratch = pltpu.VMEM((8 * (tiles + 2 * PAD), 128), f32)
    return pl.pallas_call(
        functools.partial(place_kernel, lats=lats, lons=lons),
        out_shape=jax.ShapeDtypeStruct((lats * lons, 8, 128), f32),
        in_specs=[smem, smem] + [vmem] * 5,
        out_specs=vmem,
        scratch_shapes=[scratch, scratch],
        compiler_params=pltpu.CompilerParams(vmem_limit_bytes=16 * 1024 * 1024),
        cost_estimate=pl.CostEstimate(flops=4_000_000_000, bytes_accessed=4_000_000, transcendentals=0),
        name="place",
    )(round_index, limits, *columns)


def untouched(shape):
    return pl.pallas_call(
        lambda ref: None,
        out_shape=jax.ShapeDtypeStruct(shape, f32),
        out_specs=pl.BlockSpec(memory_space=pl.ANY),
        name="untouched",
    )()


def taper(distance, kappa):
    square = distance * distance
    inside = jnp.maximum(1.0 - square * (1.0 / (RAD * RAD)), 0.0)
    return jnp.exp2(square * (-LOG2E / kappa)) * (inside * inside)


def spread(window, group_of, groups):
    tiles = [window[16 * i : 16 * i + 16] for i in range(window.shape[0] // 16)]
    wide = jnp.broadcast_to(group_of, (16, 128))
    zero = jnp.zeros((16, 128), bf16)
    hits = [wide == float(g) for g in range(1 - len(tiles), groups)]
    out = []
    for g in range(groups):
        value = zero
        for i in range(len(tiles)):
            value = jnp.where(hits[g - i + len(tiles) - 1], tiles[i], value)
        out.append(value)
    return jnp.concatenate(out, axis=0)


def analyse_kernel(
    extra_count, arrived_ref, more_ref, mid_ref, north_ref, south_ref, out_ref,
    table, dep_ref, field_ref, lhs_ref, acc_ref, left_ref, window_ref, bounds, extra_ref, sem,
):
    sources = arrived_ref.shape[0]
    sources = sources // 8
    slot_line = lax.broadcasted_iota(jnp.int32, (CAP, sources), 0)

    def load_round(src, first):
        turned = [jnp.transpose(src[pl.ds(i, sources, stride=8), :]) for i in range(8)]
        for i in range(5):
            table[i, pl.ds(first, 128), :] = turned[i]
            half = 64 * (i % 2)
            table[i, pl.ds(first + 128, 64), :] = turned[5 + i // 2][half : half + 64]
        there = table[0, pl.ds(first, CAP), :] > 0.0
        return jnp.max(jnp.where(there, slot_line + 1, 0))

    used = load_round(arrived_ref, 0)
    extra = extra_count[0]

    def more_rounds(k, used):
        copy = pltpu.make_async_copy(more_ref.at[k], extra_ref, sem)
        copy.start()
        copy.wait()
        count = load_round(extra_ref, pl.multiple_of((k + 1) * CAP, 64))
        return jnp.where(count > 0, (k + 1) * CAP + count, used)

    used = lax.fori_loop(0, extra, more_rounds, used)
    chunks = (used + 7) // 8

    field_ref[0:MARGIN] = north_ref[...]
    field_ref[MARGIN : MARGIN + TH] = mid_ref[...]
    field_ref[MARGIN + TH :] = south_ref[...]

    def rows8(i, k):
        first = k * 8 if isinstance(k, int) else pl.multiple_of(k * 8, 8)
        return table[i, pl.ds(first, 8), :]

    def find_bounds(k, carry):
        there = rows8(0, k) > 0.0
        col = rows8(1, k) + (COL_CODE + MARGIN)
        bounds[0, k] = jnp.min(jnp.where(there, col, 511.0)).astype(jnp.int32)
        bounds[1, k] = jnp.max(jnp.where(there, col, 0.0)).astype(jnp.int32)
        return carry

    for k in range(CAP // 8):
        find_bounds(k, 0)
    lax.fori_loop(CAP // 8, chunks, find_bounds, 0)
    for i in range(5):
        table[i, pl.ds(pl.multiple_of(chunks * 8, 8), 8), :] = jnp.zeros((8, sources), f32)
    bounds[0, chunks] = 0
    bounds[1, chunks] = 0

    line8 = lax.broadcasted_iota(jnp.int32, (8, 128), 0).astype(f32)
    line256 = lax.broadcasted_iota(jnp.int32, (256, 128), 0).astype(f32).astype(bf16)
    zeros = jnp.zeros((256, 128), bf16)
    line32 = lax.broadcasted_iota(jnp.int32, (32, 128), 0).astype(f32)
    empty8 = jnp.zeros((8, 128), f32)

    def aligned(window, late):
        late = jnp.broadcast_to(late, (8, 128)) > 0.0
        tiles = [empty8] + [window[8 * i : 8 * i + 8] for i in range(4)] + [empty8]
        moved = [jnp.where(late, tiles[i], tiles[i + 1]) for i in range(5)] + [empty8]
        return jnp.concatenate(moved, axis=0).astype(bf16)

    def start_of(position):
        eighth = jnp.floor((position - (RAD - 1.0)) * 0.125)
        group = jnp.floor(eighth * 0.5)
        return group, eighth - 2.0 * group, 8.0 * eighth - position

    def prepare(first_row, height):
        field = field_ref[first_row : first_row + height]
        high = field.astype(bf16)
        low = (field - high.astype(f32)).astype(bf16)
        empty = jnp.zeros((height, 128), bf16)
        for i, split in enumerate((high, low, high)):
            for b in range(4):
                piece = split[:, 128 * b : 128 * b + 128]
                lhs_ref[b, 0:height, 256 * i : 256 * i + 128] = piece
                if b > 0:
                    lhs_ref[b - 1, 0:height, 256 * i + 128 : 256 * i + 256] = piece
            lhs_ref[3, 0:height, 256 * i + 128 : 256 * i + 256] = empty

    def both_parts(x):
        high = x.astype(bf16)
        return high, (x - high.astype(f32)).astype(bf16)

    def interpolate(k, block, first_row, height):
        groups = height // 8
        row = rows8(0, k) + (MARGIN - ROW_CODE - first_row)
        off = rows8(1, k) + (COL_CODE + MARGIN) - (block * 128).astype(f32)
        frac_row = rows8(2, k)
        frac_col = rows8(3, k)
        group = jnp.floor(row * 0.125)
        below = row - 8.0 * group
        here, after = both_parts(1.0 - frac_col), both_parts(frac_col)
        next_off = (off + 1.0).astype(bf16)
        off = off.astype(bf16)
        mixes = ([], [])
        for j in range(8):
            one = slice(j, j + 1)
            at_col = jnp.broadcast_to(off[one], (256, 128)) == line256
            at_next = jnp.broadcast_to(next_off[one], (256, 128)) == line256
            for part in range(2):
                mixes[part].append(
                    jnp.where(
                        at_col,
                        jnp.broadcast_to(here[part][one], (256, 128)),
                        jnp.where(at_next, jnp.broadcast_to(after[part][one], (256, 128)), zeros),
                    )
                )
        high = jnp.concatenate(mixes[0], axis=1)
        low = jnp.concatenate(mixes[1], axis=1)
        lines = jnp.dot(
            lhs_ref[block, 0:height],
            jnp.concatenate([high, high, low], axis=0),
            preferred_element_type=f32,
        )
        out = []
        for j in range(8):
            mine = lines[:, 128 * j : 128 * j + 128]
            which = jnp.broadcast_to(group[j : j + 1], (8, 128))
            same = jnp.zeros((8, 128), f32)
            following = jnp.zeros((8, 128), f32)
            for g in range(groups):
                hit = which == float(g)
                same = jnp.where(hit, mine[8 * g : 8 * g + 8], same)
                if g + 1 < groups:
                    following = jnp.where(hit, mine[8 * g + 8 : 8 * g + 16], following)
            fy = frac_row[j : j + 1]
            near = line8 - jnp.broadcast_to(below[j : j + 1], (8, 128))
            weight_a = jnp.where(near == 0.0, 1.0 - fy, jnp.where(near == 1.0, fy, 0.0))
            weight_b = jnp.where(near == -7.0, fy, 0.0)
            out.append(jnp.sum(weight_a * same + weight_b * following, axis=0, keepdims=True))
        return jnp.concatenate(out, axis=0)

    def at8(k):
        return pl.ds(pl.multiple_of(k * 8, 8), 8)

    def low_block(k):
        return lax.shift_right_logical(bounds[0, k], 7)

    def depart(k, first_row, height):
        dep_ref[at8(k), :] = rows8(4, k) - interpolate(k, low_block(k), first_row, height)

    def depart_rest(k, first_row, height):
        def pair(w, carry):
            block = low_block(k) + 2 * w
            dep_ref[at8(k), :] -= interpolate(k, block, first_row, height)
            return carry

        high_block = lax.shift_right_logical(bounds[1, k] + 1, 7)
        lax.fori_loop(1, lax.shift_right_logical(high_block - low_block(k), 1) + 1, pair, 0)

    def first_window(k):
        return lax.shift_right_logical(jnp.maximum(bounds[0, k] - (RAD - 1), 0), 7)

    def add_window(left, col_windows, col_group, block, height):
        shifted = col_group - (block * 8).astype(f32)
        right = jnp.concatenate(
            [spread(col_windows[j], shifted[j : j + 1].astype(bf16), 16) for j in range(8)], axis=1
        )
        both = lax.dot_general(left, right, (((1,), (1,)), ((), ())), preferred_element_type=f32)
        acc_ref[block, 0:height] += both[:, 0:128]
        acc_ref[block + 1, 0:height] += both[:, 128:256]

    def column_parts(k):
        col = rows8(1, k) + (COL_CODE + MARGIN)
        return start_of(col)

    def add_sums(k, kappa, row_shift, groups):
        dep = dep_ref[at8(k), :]
        row = rows8(0, k) + (row_shift - ROW_CODE)
        frac_row = rows8(2, k)
        frac_col = rows8(3, k)
        row_group, row_late, row_from = start_of(row)
        col_group, col_late, col_from = column_parts(k)
        left = []
        col_windows = []
        for j in range(8):
            gap = (line32 + row_from[j : j + 1]) - frac_row[j : j + 1]
            weight = taper(gap, kappa)
            which = row_group[j : j + 1].astype(bf16)
            late = row_late[j : j + 1]
            numer = spread(aligned(weight * dep[j : j + 1], late), which, groups)
            denom = spread(aligned(weight, late), which, groups)
            left.append(jnp.concatenate([numer, denom], axis=0))
            gap = (line32 + col_from[j : j + 1]) - frac_col[j : j + 1]
            col_windows.append(aligned(taper(gap, kappa), col_late[j : j + 1]))
        left = jnp.concatenate(left, axis=1)
        height = 32 * groups
        left_ref[0:height] = left
        for j in range(8):
            window_ref[j] = col_windows[j]
        add_window(left_ref[0:height], col_windows, col_group, first_window(k), height)

    def add_rest(k, groups):
        height = 32 * groups

        def pair(w, carry):
            col_group = column_parts(k)[0]
            windows = [window_ref[j] for j in range(8)]
            add_window(left_ref[0:height], windows, col_group, first_window(k) + 2 * w, height)
            return carry

        last = lax.shift_right_logical(jnp.minimum(bounds[1, k] + RAD, LANES - 1), 7)
        lax.fori_loop(1, lax.shift_right_logical(last - first_window(k), 1) + 1, pair, 0)

    def one_pass(kappa, first_row, field_height, row_shift, groups):
        prepare(first_row, field_height)
        acc_ref[...] = jnp.zeros_like(acc_ref)

        def ahead(k, carry):
            depart(k, first_row, field_height)
            depart_rest(k, first_row, field_height)
            return carry

        lax.fori_loop(0, jnp.minimum(chunks, 1), ahead, 0)

        def chunk(k, carry):
            following = jnp.minimum(k + 1, chunks)
            add_sums(k, kappa, row_shift, groups)
            depart(following, first_row, field_height)
            add_rest(k, groups)
            depart_rest(following, first_row, field_height)
            return carry

        lax.fori_loop(0, chunks, chunk, 0)

    one_pass(KAPPA_ONE, 0, EXT_ROWS, 16.0, 10)
    field_ref[0:8] = jnp.zeros((8, LANES), f32)
    field_ref[168:EXT_ROWS] = jnp.zeros((8, LANES), f32)
    for b in range(4):
        lanes = slice(128 * b, 128 * b + 128)
        field_ref[8:168, lanes] += acc_ref[b, 0:160] / (acc_ref[b, 160:320] + 1.0)
    one_pass(KAPPA_TWO, 8, 160, 0.0, 8)
    final = jnp.concatenate(
        [
            field_ref[MARGIN : MARGIN + TH, 128 * b : 128 * b + 128]
            + acc_ref[b, 0:TH] / (acc_ref[b, TH : 2 * TH] + 1.0)
            for b in range(4)
        ],
        axis=1,
    )
    out_ref[...] = pltpu.roll(final, LANES - MARGIN, 1)[:, 0:TW]


def analyse(extra, arrived, more, middle, north, south):
    vmem = pl.BlockSpec(memory_space=pltpu.VMEM)
    sources = arrived.shape[0]
    slots = ROUNDS * CAP
    return pl.pallas_call(
        analyse_kernel,
        out_shape=jax.ShapeDtypeStruct((TH, TW), f32),
        in_specs=[pl.BlockSpec(memory_space=pltpu.SMEM), vmem, pl.BlockSpec(memory_space=pl.ANY), vmem, vmem, vmem],
        out_specs=vmem,
        scratch_shapes=[
            pltpu.VMEM((5, slots + 8, sources), f32),
            pltpu.VMEM((slots + 8, sources), f32),
            pltpu.VMEM((EXT_ROWS, LANES), f32),
            pltpu.VMEM((4, EXT_ROWS, 768), bf16),
            pltpu.VMEM((5, 320, 128), f32),
            pltpu.VMEM((320, 8 * sources), bf16),
            pltpu.VMEM((8, 48, sources), bf16),
            pltpu.SMEM((2, slots // 8 + 1), jnp.int32),
            pltpu.VMEM((sources * 8, 128), f32),
            pltpu.SemaphoreType.DMA,
        ],
        compiler_params=pltpu.CompilerParams(vmem_limit_bytes=48 * 1024 * 1024),
        name="analyse",
    )(extra.reshape(1), arrived.reshape(sources * 8, 128), more, middle, north, south)


def on_device(background, obs_cell, obs_frac, obs_value):
    lats = lax.axis_size("lat")
    lons = lax.axis_size("lon")
    axes = ("lat", "lon")
    devices = lats * lons

    west = neighbour(background, "lon", 1, True)[:, TW - MARGIN :]
    east = neighbour(background, "lon", -1, True)[:, :MARGIN]
    spare = jnp.zeros((TH, LANES - TW - 2 * MARGIN), f32)
    middle = jnp.concatenate([west, background, east, spare], axis=1)

    columns = sort_observations(obs_cell, obs_frac, obs_value, lats)
    columns, middle = lax.optimization_barrier((columns, middle))
    limits = segment_limits(columns[0], lats, lons)

    def outgoing(k):
        return place(k.reshape(1), limits, *columns, lats, lons)

    def exchange(block):
        return lax.all_to_all(block, axes, split_axis=0, concat_axis=0, tiled=True)

    first, middle = lax.optimization_barrier((outgoing(jnp.int32(0)), middle))
    arrived = exchange(first)
    north = neighbour(middle[TH - MARGIN :], "lat", 1, False)
    south = neighbour(middle[:MARGIN], "lat", -1, False)
    extra = jnp.max(arrived[:, 7, 127]).astype(jnp.int32)

    def one_more(k, held):
        got = exchange(outgoing(k + 1)).reshape(1, devices * 8, 128)
        return lax.dynamic_update_slice_in_dim(held, got, k, 0)

    more = lax.fori_loop(0, extra, one_more, untouched((ROUNDS - 1, devices * 8, 128)))
    return analyse(extra, arrived, more, middle, north, south)


def solution(mesh):
    placed = (P("lat", "lon"), P(None, ("lat", "lon")), P(None, ("lat", "lon")), P(("lat", "lon")))
    return jax.shard_map(
        on_device, mesh=mesh, in_specs=placed, out_specs=P("lat", "lon"), check_vma=False
    )
```

```python
import functools

import jax
import jax.numpy as jnp
from jax import lax
from jax.experimental import pallas as pl
from jax.experimental.pallas import tpu as pltpu
from jax.sharding import PartitionSpec as P

RAD = 12
MARGIN = 24
TH = 128
TW = 384
CAP = 192
ROUNDS = 6
BAND = 8192
NOWHERE = 1 << 30
PAD = 4
EXT_ROWS = TH + 2 * MARGIN
LANES = 512
ROW_CODE = 64.0
COL_CODE = 192.0
LOG2E = 1.4426950408889634
KAPPA_ONE = RAD * RAD / 9.0
KAPPA_TWO = 0.35 * KAPPA_ONE
f32 = jnp.float32
bf16 = jnp.bfloat16


def neighbour(block, axis, distance, wrap):
    count = lax.axis_size(axis)
    route = [(i, (i + distance) % count) for i in range(count) if wrap or 0 <= i + distance < count]
    return lax.ppermute(block, axis, route)


def key_kernel(cell_ref, frac_ref, value_ref, key_ref, rows_ref, fy_ref, fx_ref, out_ref, row_ref, col_ref, *, lats):
    half = row_ref.shape[0]
    for i in range(half):
        lanes = slice(128 * i, 128 * i + 128)
        line = slice(i, i + 1)
        row_ref[line] = cell_ref[0:1, lanes]
        col_ref[line] = cell_ref[1:2, lanes]
        fy_ref[line] = frac_ref[0:1, lanes]
        fx_ref[line] = frac_ref[1:2, lanes]
        out_ref[line] = value_ref[0:1, lanes]
    for ref in (fy_ref, fx_ref, out_ref):
        ref[half : 2 * half] = ref[0:half]
    row = row_ref[...]
    lat = lax.shift_right_logical(row, 7)
    local_row = row - lat * TH
    up = (local_row <= MARGIN - 2) & (lat > 0)
    down = (local_row >= TH - MARGIN) & (lat < lats - 1)
    move = jnp.where(up, -1, jnp.where(down, 1, 0))
    own_key = lat * BAND + col_ref[...]
    key_ref[0:half] = own_key
    key_ref[half : 2 * half] = jnp.where(move == 0, NOWHERE, own_key + move * BAND)
    rows_ref[0:half] = local_row.astype(f32) + ROW_CODE
    rows_ref[half : 2 * half] = (local_row - move * TH).astype(f32) + ROW_CODE


def sort_observations(obs_cell, obs_frac, obs_value, lats):
    vmem = pl.BlockSpec(memory_space=pltpu.VMEM)
    half = obs_value.shape[0] // 128
    whole = jax.ShapeDtypeStruct((2 * half, 128), f32)
    scratch = pltpu.VMEM((half, 128), jnp.int32)
    columns = pl.pallas_call(
        functools.partial(key_kernel, lats=lats),
        out_shape=[jax.ShapeDtypeStruct((2 * half, 128), jnp.int32)] + [whole] * 4,
        in_specs=[vmem] * 3,
        out_specs=[vmem] * 5,
        scratch_shapes=[scratch, scratch],
        name="keys",
    )(obs_cell, obs_frac, obs_value[None, :])
    return lax.sort([x.reshape(256 * half) for x in columns], num_keys=1, is_stable=False)


def segment_limits(keys, lats, lons):
    low = [TW * b - MARGIN for b in range(lons)]
    high = [TW * (b + 1) + MARGIN - 1 for b in range(lons)]
    total = TW * lons
    band = low + high + [0, total]
    band[0] += total
    band[2 * lons - 1] -= total
    limits = jnp.array([a * BAND + x for a in range(lats) for x in band], jnp.int32)
    return jnp.sum((keys[None, :] < limits[:, None]).astype(jnp.int32), axis=1)


def pieces_of(limit_ref, a, b, lons):
    base = a * (2 * lons + 2)
    first = limit_ref[base + b]
    end = limit_ref[base + lons + b]
    if b == 0:
        return (first, limit_ref[base + 2 * lons + 1]), (limit_ref[base + 2 * lons], end)
    if b == lons - 1:
        return (first, limit_ref[base + 2 * lons + 1]), (limit_ref[base + 2 * lons], end)
    return (first, end), None


def place_kernel(round_ref, limit_ref, key_ref, row_ref, fy_ref, fx_ref, value_ref, out_ref, near_ref, far_ref, *, lats, lons):
    tiles = key_ref.shape[0]
    skipped = round_ref[0] * CAP
    col = (key_ref[...] & (BAND - 1)).astype(f32)
    near = [row_ref[...], col, fy_ref[...], fx_ref[...], value_ref[...], row_ref[...], fy_ref[...], value_ref[...]]
    lane = lax.broadcasted_iota(jnp.int32, (8, 128), 1)
    line = lax.broadcasted_iota(jnp.int32, (8, 128), 0)
    for i, x in enumerate(near):
        near_ref[pl.ds(8 * PAD + i, tiles, stride=8), :] = x
    for i, x in ((5, col), (6, fx_ref[...])):
        far_ref[pl.ds(8 * PAD + i, tiles, stride=8), :] = x
    entry = jnp.where(line < 5, lane, 128 + (lane & 63))
    col_line = (line == 1) | ((line == 5) & (lane >= 64))
    meta = (line == 7) & (lane >= 64)

    def window(ref, tile, start):
        return ref[pl.ds(pl.multiple_of(tile * 8, 8), 8), :]

    def take(start):
        start = jnp.clip(start + 128 * PAD, 0, (tiles + PAD) * 128)
        tile = lax.shift_right_logical(start, 7)
        inside = start & 127
        turn = (128 - inside) & 127
        views = [pltpu.roll(window(near_ref, tile + i, 0), turn, 1) for i in range(3)]
        kept = lane < 128 - inside
        first = jnp.where(kept, views[0], views[1])
        second = jnp.where(kept, views[1], views[2])
        start = start + 64
        tile = lax.shift_right_logical(start, 7)
        inside = start & 127
        turn = (128 - inside) & 127
        views = [pltpu.roll(window(far_ref, tile + i, 0), turn, 1) for i in range(2)]
        third = jnp.where(lane < 128 - inside, views[0], views[1])
        return jnp.where(line < 5, first, jnp.where(lane < 64, second, third))

    def band(a, most):
        for b in range(lons):
            one, two = pieces_of(limit_ref, a, b, lons)
            count = one[1] - one[0] - skipped
            shift = -float(TW * b) - COL_CODE
            value = take(one[0] + skipped)
            if two is None:
                value = value + jnp.where(col_line, shift, 0.0)
            else:
                total = float(TW * lons)
                first_shift, second_shift = (shift - total, shift) if b == 0 else (shift, shift + total)
                value = value + jnp.where(col_line, first_shift, 0.0)
                other = take(two[0] - count) + jnp.where(col_line, second_shift, 0.0)
                value = jnp.where(entry < count, value, other)
                count = count + two[1] - two[0]
            most = jnp.maximum(most, count)
            out_ref[a * lons + b] = jnp.where((entry < count) & ~meta, value, 0.0)
        return most

    most = lax.fori_loop(0, lats, band, 0)
    extra = jnp.maximum(most + (CAP - 1), 0) // CAP - 1
    extra = jnp.maximum(extra, 0).astype(f32)

    flags = jnp.full((1, 64), extra, f32)
    for t in range(lats * lons):
        out_ref[t, 7:8, 64:128] = flags


def place(round_index, limits, keys, rows, fy, fx, values, lats, lons):
    vmem = pl.BlockSpec(memory_space=pltpu.VMEM)
    smem = pl.BlockSpec(memory_space=pltpu.SMEM)
    tiles = keys.shape[0] // 128
    columns = [x.reshape(tiles, 128) for x in (keys, rows, fy, fx, values)]
    scratch = pltpu.VMEM((8 * (tiles + 2 * PAD), 128), f32)
    return pl.pallas_call(
        functools.partial(place_kernel, lats=lats, lons=lons),
        out_shape=jax.ShapeDtypeStruct((lats * lons, 8, 128), f32),
        in_specs=[smem, smem] + [vmem] * 5,
        out_specs=vmem,
        scratch_shapes=[scratch, scratch],
        compiler_params=pltpu.CompilerParams(vmem_limit_bytes=16 * 1024 * 1024),
        cost_estimate=pl.CostEstimate(flops=4_000_000_000, bytes_accessed=4_000_000, transcendentals=0),
        name="place",
    )(round_index, limits, *columns)


def untouched(shape):
    return pl.pallas_call(
        lambda ref: None,
        out_shape=jax.ShapeDtypeStruct(shape, f32),
        out_specs=pl.BlockSpec(memory_space=pl.ANY),
        name="untouched",
    )()


def taper(distance, kappa):
    square = distance * distance
    inside = jnp.maximum(1.0 - square * (1.0 / (RAD * RAD)), 0.0)
    return jnp.exp2(square * (-LOG2E / kappa)) * (inside * inside)


def spread(window, group_of, groups):
    tiles = [window[16 * i : 16 * i + 16] for i in range(window.shape[0] // 16)]
    wide = jnp.broadcast_to(group_of, (16, 128))
    zero = jnp.zeros((16, 128), bf16)
    hits = [wide == float(g) for g in range(1 - len(tiles), groups)]
    out = []
    for g in range(groups):
        value = zero
        for i in range(len(tiles)):
            value = jnp.where(hits[g - i + len(tiles) - 1], tiles[i], value)
        out.append(value)
    return jnp.concatenate(out, axis=0)


def analyse_kernel(
    extra_count, arrived_ref, more_ref, mid_ref, north_ref, south_ref, out_ref,
    table, dep_ref, field_ref, lhs_ref, acc_ref, left_ref, window_ref, bounds, extra_ref, sem,
):
    sources = arrived_ref.shape[0]
    sources = sources // 8
    slot_line = lax.broadcasted_iota(jnp.int32, (CAP, sources), 0)

    def load_round(src, first):
        turned = [jnp.transpose(src[pl.ds(i, sources, stride=8), :]) for i in range(8)]
        for i in range(5):
            table[i, pl.ds(first, 128), :] = turned[i]
            half = 64 * (i % 2)
            table[i, pl.ds(first + 128, 64), :] = turned[5 + i // 2][half : half + 64]
        there = table[0, pl.ds(first, CAP), :] > 0.0
        return jnp.max(jnp.where(there, slot_line + 1, 0))

    used = load_round(arrived_ref, 0)
    extra = extra_count[0]

    def more_rounds(k, used):
        copy = pltpu.make_async_copy(more_ref.at[k], extra_ref, sem)
        copy.start()
        copy.wait()
        count = load_round(extra_ref, pl.multiple_of((k + 1) * CAP, 64))
        return jnp.where(count > 0, (k + 1) * CAP + count, used)

    used = lax.fori_loop(0, extra, more_rounds, used)
    chunks = (used + 7) // 8

    field_ref[0:MARGIN] = north_ref[...]
    field_ref[MARGIN : MARGIN + TH] = mid_ref[...]
    field_ref[MARGIN + TH :] = south_ref[...]

    def rows8(i, k):
        first = k * 8 if isinstance(k, int) else pl.multiple_of(k * 8, 8)
        return table[i, pl.ds(first, 8), :]

    def find_bounds(k, carry):
        there = rows8(0, k) > 0.0
        col = rows8(1, k) + (COL_CODE + MARGIN)
        bounds[0, k] = jnp.min(jnp.where(there, col, 511.0)).astype(jnp.int32)
        bounds[1, k] = jnp.max(jnp.where(there, col, 0.0)).astype(jnp.int32)
        return carry

    for k in range(CAP // 8):
        find_bounds(k, 0)
    lax.fori_loop(CAP // 8, chunks, find_bounds, 0)
    for i in range(5):
        table[i, pl.ds(pl.multiple_of(chunks * 8, 8), 8), :] = jnp.zeros((8, sources), f32)
    bounds[0, chunks] = 0
    bounds[1, chunks] = 0

    line8 = lax.broadcasted_iota(jnp.int32, (8, 128), 0).astype(f32)
    line256 = lax.broadcasted_iota(jnp.int32, (256, 128), 0).astype(f32).astype(bf16)
    zeros = jnp.zeros((256, 128), bf16)
    line32 = lax.broadcasted_iota(jnp.int32, (32, 128), 0).astype(f32)
    empty8 = jnp.zeros((8, 128), f32)

    def aligned(window, late):
        late = jnp.broadcast_to(late, (8, 128)) > 0.0
        tiles = [empty8] + [window[8 * i : 8 * i + 8] for i in range(4)] + [empty8]
        moved = [jnp.where(late, tiles[i], tiles[i + 1]) for i in range(5)] + [empty8]
        return jnp.concatenate(moved, axis=0).astype(bf16)

    def start_of(position):
        eighth = jnp.floor((position - (RAD - 1.0)) * 0.125)
        group = jnp.floor(eighth * 0.5)
        return group, eighth - 2.0 * group, 8.0 * eighth - position

    def prepare(first_row, height):
        field = field_ref[first_row : first_row + height]
        high = field.astype(bf16)
        low = (field - high.astype(f32)).astype(bf16)
        empty = jnp.zeros((height, 128), bf16)
        for i, split in enumerate((high, low, high)):
            for b in range(4):
                piece = split[:, 128 * b : 128 * b + 128]
                lhs_ref[b, 0:height, 256 * i : 256 * i + 128] = piece
                if b > 0:
                    lhs_ref[b - 1, 0:height, 256 * i + 128 : 256 * i + 256] = piece
            lhs_ref[3, 0:height, 256 * i + 128 : 256 * i + 256] = empty

    def both_parts(x):
        high = x.astype(bf16)
        return high, (x - high.astype(f32)).astype(bf16)

    def interpolate(k, block, first_row, height):
        groups = height // 8
        row = rows8(0, k) + (MARGIN - ROW_CODE - first_row)
        off = rows8(1, k) + (COL_CODE + MARGIN) - (block * 128).astype(f32)
        frac_row = rows8(2, k)
        frac_col = rows8(3, k)
        group = jnp.floor(row * 0.125)
        below = row - 8.0 * group
        here, after = both_parts(1.0 - frac_col), both_parts(frac_col)
        next_off = (off + 1.0).astype(bf16)
        off = off.astype(bf16)
        mixes = ([], [])
        for j in range(8):
            one = slice(j, j + 1)
            at_col = jnp.broadcast_to(off[one], (256, 128)) == line256
            at_next = jnp.broadcast_to(next_off[one], (256, 128)) == line256
            for part in range(2):
                mixes[part].append(
                    jnp.where(
                        at_col,
                        jnp.broadcast_to(here[part][one], (256, 128)),
                        jnp.where(at_next, jnp.broadcast_to(after[part][one], (256, 128)), zeros),
                    )
                )
        high = jnp.concatenate(mixes[0], axis=1)
        low = jnp.concatenate(mixes[1], axis=1)
        lines = jnp.dot(
            lhs_ref[block, 0:height, 0:512],
            jnp.concatenate([high, high], axis=0),
            preferred_element_type=f32,
        ) + jnp.dot(lhs_ref[block, 0:height, 512:768], low, preferred_element_type=f32)
        out = []
        for j in range(8):
            mine = lines[:, 128 * j : 128 * j + 128]
            which = jnp.broadcast_to(group[j : j + 1], (8, 128))
            same = jnp.zeros((8, 128), f32)
            following = jnp.zeros((8, 128), f32)
            for g in range(groups):
                hit = which == float(g)
                same = jnp.where(hit, mine[8 * g : 8 * g + 8], same)
                if g + 1 < groups:
                    following = jnp.where(hit, mine[8 * g + 8 : 8 * g + 16], following)
            fy = frac_row[j : j + 1]
            near = line8 - jnp.broadcast_to(below[j : j + 1], (8, 128))
            weight_a = jnp.where(near == 0.0, 1.0 - fy, jnp.where(near == 1.0, fy, 0.0))
            weight_b = jnp.where(near == -7.0, fy, 0.0)
            out.append(jnp.sum(weight_a * same + weight_b * following, axis=0, keepdims=True))
        return jnp.concatenate(out, axis=0)

    def at8(k):
        return pl.ds(pl.multiple_of(k * 8, 8), 8)

    def low_block(k):
        return lax.shift_right_logical(bounds[0, k], 7)

    def depart(k, first_row, height):
        dep_ref[at8(k), :] = rows8(4, k) - interpolate(k, low_block(k), first_row, height)

    def depart_rest(k, first_row, height):
        def pair(w, carry):
            block = low_block(k) + 2 * w
            dep_ref[at8(k), :] -= interpolate(k, block, first_row, height)
            return carry

        high_block = lax.shift_right_logical(bounds[1, k] + 1, 7)
        lax.fori_loop(1, lax.shift_right_logical(high_block - low_block(k), 1) + 1, pair, 0)

    def first_window(k):
        return lax.shift_right_logical(jnp.maximum(bounds[0, k] - (RAD - 1), 0), 7)

    def add_window(left, col_windows, col_group, block, height):
        shifted = col_group - (block * 8).astype(f32)
        right = jnp.concatenate(
            [spread(col_windows[j], shifted[j : j + 1].astype(bf16), 16) for j in range(8)], axis=1
        )
        both = lax.dot_general(left, right, (((1,), (1,)), ((), ())), preferred_element_type=f32)
        acc_ref[block, 0:height] += both[:, 0:128]
        acc_ref[block + 1, 0:height] += both[:, 128:256]

    def column_parts(k):
        col = rows8(1, k) + (COL_CODE + MARGIN)
        return start_of(col)

    def add_sums(k, kappa, row_shift, groups):
        dep = dep_ref[at8(k), :]
        row = rows8(0, k) + (row_shift - ROW_CODE)
        frac_row = rows8(2, k)
        frac_col = rows8(3, k)
        row_group, row_late, row_from = start_of(row)
        col_group, col_late, col_from = column_parts(k)
        left = []
        col_windows = []
        for j in range(8):
            gap = (line32 + row_from[j : j + 1]) - frac_row[j : j + 1]
            weight = taper(gap, kappa)
            which = row_group[j : j + 1].astype(bf16)
            late = row_late[j : j + 1]
            numer = spread(aligned(weight * dep[j : j + 1], late), which, groups)
            denom = spread(aligned(weight, late), which, groups)
            left.append(jnp.concatenate([numer, denom], axis=0))
            gap = (line32 + col_from[j : j + 1]) - frac_col[j : j + 1]
            col_windows.append(aligned(taper(gap, kappa), col_late[j : j + 1]))
        left = jnp.concatenate(left, axis=1)
        height = 32 * groups
        left_ref[0:height] = left
        for j in range(8):
            window_ref[j] = col_windows[j]
        add_window(left_ref[0:height], col_windows, col_group, first_window(k), height)

    def add_rest(k, groups):
        height = 32 * groups

        def pair(w, carry):
            col_group = column_parts(k)[0]
            windows = [window_ref[j] for j in range(8)]
            add_window(left_ref[0:height], windows, col_group, first_window(k) + 2 * w, height)
            return carry

        last = lax.shift_right_logical(jnp.minimum(bounds[1, k] + RAD, LANES - 1), 7)
        lax.fori_loop(1, lax.shift_right_logical(last - first_window(k), 1) + 1, pair, 0)

    def one_pass(kappa, first_row, field_height, row_shift, groups):
        prepare(first_row, field_height)
        acc_ref[...] = jnp.zeros_like(acc_ref)

        def ahead(k, carry):
            depart(k, first_row, field_height)
            depart_rest(k, first_row, field_height)
            return carry

        lax.fori_loop(0, jnp.minimum(chunks, 1), ahead, 0)

        def chunk(k, carry):
            following = jnp.minimum(k + 1, chunks)
            add_sums(k, kappa, row_shift, groups)
            depart(following, first_row, field_height)
            add_rest(k, groups)
            depart_rest(following, first_row, field_height)
            return carry

        lax.fori_loop(0, chunks, chunk, 0)

    one_pass(KAPPA_ONE, 0, EXT_ROWS, 16.0, 10)
    field_ref[0:8] = jnp.zeros((8, LANES), f32)
    field_ref[168:EXT_ROWS] = jnp.zeros((8, LANES), f32)
    for b in range(4):
        lanes = slice(128 * b, 128 * b + 128)
        field_ref[8:168, lanes] += acc_ref[b, 0:160] / (acc_ref[b, 160:320] + 1.0)
    one_pass(KAPPA_TWO, 8, 160, 0.0, 8)
    final = jnp.concatenate(
        [
            field_ref[MARGIN : MARGIN + TH, 128 * b : 128 * b + 128]
            + acc_ref[b, 0:TH] / (acc_ref[b, TH : 2 * TH] + 1.0)
            for b in range(4)
        ],
        axis=1,
    )
    out_ref[...] = pltpu.roll(final, LANES - MARGIN, 1)[:, 0:TW]


def analyse(extra, arrived, more, middle, north, south):
    vmem = pl.BlockSpec(memory_space=pltpu.VMEM)
    sources = arrived.shape[0]
    slots = ROUNDS * CAP
    return pl.pallas_call(
        analyse_kernel,
        out_shape=jax.ShapeDtypeStruct((TH, TW), f32),
        in_specs=[pl.BlockSpec(memory_space=pltpu.SMEM), vmem, pl.BlockSpec(memory_space=pl.ANY), vmem, vmem, vmem],
        out_specs=vmem,
        scratch_shapes=[
            pltpu.VMEM((5, slots + 8, sources), f32),
            pltpu.VMEM((slots + 8, sources), f32),
            pltpu.VMEM((EXT_ROWS, LANES), f32),
            pltpu.VMEM((4, EXT_ROWS, 768), bf16),
            pltpu.VMEM((5, 320, 128), f32),
            pltpu.VMEM((320, 8 * sources), bf16),
            pltpu.VMEM((8, 48, sources), bf16),
            pltpu.SMEM((2, slots // 8 + 1), jnp.int32),
            pltpu.VMEM((sources * 8, 128), f32),
            pltpu.SemaphoreType.DMA,
        ],
        compiler_params=pltpu.CompilerParams(vmem_limit_bytes=48 * 1024 * 1024),
        name="analyse",
    )(extra.reshape(1), arrived.reshape(sources * 8, 128), more, middle, north, south)


def on_device(background, obs_cell, obs_frac, obs_value):
    lats = lax.axis_size("lat")
    lons = lax.axis_size("lon")
    axes = ("lat", "lon")
    devices = lats * lons

    west = neighbour(background, "lon", 1, True)[:, TW - MARGIN :]
    east = neighbour(background, "lon", -1, True)[:, :MARGIN]
    spare = jnp.zeros((TH, LANES - TW - 2 * MARGIN), f32)
    middle = jnp.concatenate([west, background, east, spare], axis=1)

    columns = sort_observations(obs_cell, obs_frac, obs_value, lats)
    columns, middle = lax.optimization_barrier((columns, middle))
    limits = segment_limits(columns[0], lats, lons)

    def outgoing(k):
        return place(k.reshape(1), limits, *columns, lats, lons)

    def exchange(block):
        return lax.all_to_all(block, axes, split_axis=0, concat_axis=0, tiled=True)

    first, middle = lax.optimization_barrier((outgoing(jnp.int32(0)), middle))
    arrived = exchange(first)
    north = neighbour(middle[TH - MARGIN :], "lat", 1, False)
    south = neighbour(middle[:MARGIN], "lat", -1, False)
    extra = jnp.max(arrived[:, 7, 127]).astype(jnp.int32)

    def one_more(k, held):
        got = exchange(outgoing(k + 1)).reshape(1, devices * 8, 128)
        return lax.dynamic_update_slice_in_dim(held, got, k, 0)

    more = lax.fori_loop(0, extra, one_more, untouched((ROUNDS - 1, devices * 8, 128)))
    return analyse(extra, arrived, more, middle, north, south)


def solution(mesh):
    placed = (P("lat", "lon"), P(None, ("lat", "lon")), P(None, ("lat", "lon")), P(("lat", "lon")))
    return jax.shard_map(
        on_device, mesh=mesh, in_specs=placed, out_specs=P("lat", "lon"), check_vma=False
    )
```
